32 devices in a mesh: ctx: 8 (over y, x, core), tp: 4 (over z).
Axes of the slice: x: 2, y: 2, z: 4, core: 2. Of those that a mesh axis runs over, the one named last changes fastest.
Arguments:
- queries: bfloat16 [8192, 4096], P('ctx', 'tp'), may hold values from -6 to 6
- keys: bfloat16 [8192, 4096], P('ctx', 'tp'), may hold values from -6 to 6
- values: bfloat16 [8192, 4096], P('ctx', 'tp'), may hold values from -6 to 6
- residues: float32 [16, 4096], P(None, 'tp'), may hold values from -4 to 4
- rates: float32 [16, 4096], P(None, 'tp'), may hold values from 3.0517578e-05 to 0.04
- out_weight: bfloat16 [4096, 4096], P('tp'), may hold values from -0.125 to 0.125
- span_order: int32 [16], replicated, may hold values from 0 to 15, each once
Outputs:
- projected: bfloat16 [8192, 4096], P('ctx', 'tp')
The draws below stay inside these ranges and needn't reach their ends.
Inputs may be any that keep to these rules, and one draw needn't show every extreme that they name: span_order holds each of 0 .. 15 once.
All inputs are finite; a program needn't handle non-finite values.
Results may differ from the reference program's by a relative error of at most 0.015.
Values may be sent and summed in bfloat16 or wider, within the bound.
No kernel may reach another device: no remote copies, remote signals or barrier semaphores. Data moves between devices by JAX's collectives and lax.ppermute only.
A program may use at most 128 MiB of HBM per device.

```python
import math
import jax
import jax.numpy as jnp
from jax import lax

D = 4096
MODES = 16
BLK = 64
SEQ = 8192
NCHUNK = 16
N_TP = 4


def with_spikes(result, own_key, source, target, parts, factor):
    owner, partner = [(jnp.arange(result.shape[axis_at]) // (result.shape[axis_at] // parts)).reshape([-1 if axis == axis_at else 1 for axis in range(result.ndim)]) for axis_at in (source, target)]
    chosen = jax.random.permutation(own_key, parts)[partner]
    strong = (owner == chosen) | (owner == (partner + parts // 2) % parts)
    return jnp.where(strong, factor * result, result)


def block_levels(own_key, shape, split, smallest, top_value):
    loudness, own = 1.0, jax.random.fold_in(own_key, 6)
    for position, blocks in split:
        steps = jnp.exp(jax.random.uniform(jax.random.fold_in(own, position), (blocks,), jnp.float32, smallest / len(split), top_value / len(split)))
        loudness = loudness * jnp.repeat(steps, shape[position] // blocks).reshape([-1 if axis == position else 1 for axis in range(len(shape))])
    return loudness


def centred(own_key, dims, deviation, limit, cuts=(), held_as=jnp.bfloat16):
    drawn = jax.random.normal(own_key, dims, jnp.float32) * deviation
    if len(cuts) > 0:
        drawn = block_levels(own_key, dims, cuts, -0.22, 0.18) * drawn
    return jnp.clip(drawn, min=-limit, max=limit).astype(held_as)


def bell_draw_with(key, extent, scale, most, shards, heavy, held_as=jnp.bfloat16):
    drawn = scale * jax.random.normal(key, extent, jnp.float32)
    if shards:
        drawn = drawn * block_levels(key, extent, shards, -0.22, 0.18)
    return jnp.clip(with_spikes(drawn, jax.random.fold_in(key, 3), *heavy), -most, most).astype(held_as)


def setup_inputs(seed: int = 0) -> dict:
    key_list = jax.random.split(jax.random.key(seed), 8)
    return {
        "queries": centred(key_list[0], (SEQ, D), 1.0, 6.0, ((0, 8), (1, 4))),
        "keys": centred(key_list[1], (SEQ, D), 1.0, 6.0, ((0, 8), (1, 4))),
        "values": centred(key_list[2], (SEQ, D), 1.0, 6.0, ((0, 8), (1, 4))),
        "residues": centred(key_list[3], (MODES, D), 0.25, 4.0, ((1, 4),), jnp.float32),
        "rates": jnp.clip(jnp.exp(math.log(0.04) - 7.178332 * jax.random.uniform(key_list[4], (MODES, D), jnp.float32) ** block_levels(key_list[4], (MODES, D), ((1, 4),), -0.2, 0.2)), 3.0517578125e-05, 0.04),
        "out_weight": bell_draw_with(key_list[5], (D, D), D ** -0.5, 0.125, ((0, 4),), (0, 1, 4, 2.0)),
        "span_order": jax.random.permutation(key_list[6], NCHUNK).astype(jnp.int32),
    }


def channel_mix(ordered, residues, rates):
    seq_len, width_all = ordered.shape
    group = width_all // N_TP
    nblocks = seq_len // BLK

    def one_group(index):
        start = (index * group).astype(jnp.int32)
        signal = lax.dynamic_slice_in_dim(ordered, start, group, 1).astype(jnp.float32)
        weights = lax.dynamic_slice_in_dim(residues, start, group, 1)
        decays = lax.dynamic_slice_in_dim(rates, start, group, 1)
        scaled = weights * jnp.sqrt(2.0 * decays)
        lags = jnp.arange(BLK).astype(jnp.float32)
        kernel = lax.optimization_barrier(jnp.sum(scaled[:, None, :] * jnp.exp(-decays[:, None, :] * lags[None, :, None]), axis=0))
        spread = jnp.arange(BLK)[:, None] - jnp.arange(BLK)[None, :]
        toeplitz = jnp.where((spread >= 0)[:, :, None], kernel[jnp.maximum(spread, 0)], 0.0)
        blocks = signal.reshape(nblocks, BLK, group)
        inner = jnp.einsum('tsc,nsc->ntc', toeplitz, blocks, precision=lax.Precision.HIGHEST)
        falling = jnp.exp(-decays[:, None, :] * (BLK - 1.0 - lags)[None, :, None])
        states = jnp.einsum('nsc,rsc->nrc', blocks, falling, precision=lax.Precision.HIGHEST)
        step_decay = jnp.exp(-decays * BLK)

        def advance(carry, state):
            return (step_decay * carry + state, carry)
        initial = jnp.zeros(decays.shape, jnp.float32)
        final_state, entering = lax.scan(advance, initial, states)
        rising = scaled[:, None, :] * jnp.exp(-decays[:, None, :] * (lags + 1.0)[None, :, None])
        outer = jnp.einsum('nrc,rtc->ntc', entering, rising, precision=lax.Precision.HIGHEST)
        return (inner + outer).reshape(seq_len, group)
    results = lax.map(one_group, jnp.arange(N_TP).astype(jnp.int32))
    return jnp.transpose(results, (1, 0, 2)).reshape(seq_len, width_all)

def reference(queries, keys, values, residues, rates, out_weight, span_order):
    seq_len, width_all = queries.shape
    count = span_order.shape[0]
    block_rows = seq_len // count
    gated = (keys.astype(jnp.float32) * values.astype(jnp.float32)).astype(jnp.bfloat16)
    inverse = jnp.argsort(span_order).astype(jnp.int32)
    ordered = gated.reshape(count, block_rows, width_all)[inverse].reshape(seq_len, width_all)
    convolved = channel_mix(ordered, residues, rates).astype(jnp.bfloat16)
    mixed = convolved.reshape(count, block_rows, width_all)[span_order.astype(jnp.int32)].reshape(seq_len, width_all)
    output = (queries.astype(jnp.float32) * mixed.astype(jnp.float32)).astype(jnp.bfloat16)
    group = width_all // N_TP
    out_groups = jnp.transpose(output.reshape(seq_len, N_TP, group), (1, 0, 2))
    weight_groups = out_weight.reshape(N_TP, group, width_all)

    def add_group(total, pieces):
        part = jnp.dot(pieces[0].astype(jnp.float32), pieces[1].astype(jnp.float32))
        part = lax.optimization_barrier(part.astype(jnp.bfloat16))
        return (total + part.astype(jnp.float32), None)
    total, unused = lax.scan(add_group, jnp.zeros((seq_len, width_all), jnp.float32), (out_groups, weight_groups))
    return total.astype(jnp.bfloat16)
```

```python
import functools

import jax
import jax.numpy as jnp
from jax import lax
from jax.experimental import pallas as pl
from jax.experimental.pallas import tpu as pltpu
from jax.sharding import PartitionSpec as P

ROWS = 16
LANES = 512


def gate_rows(keys_ref, values_ref, gated_ref, length):
    @pl.loop(0, length // 64)
    def _(step):
        rows = pl.ds(pl.multiple_of(step * 64, 64), 64)
        gated = keys_ref[rows, :].astype(jnp.float32) * values_ref[rows, :].astype(jnp.float32)
        gated_ref[rows, :] = gated.astype(jnp.bfloat16).astype(jnp.float32)


def states_kernel(keys_ref, values_ref, rates_ref, out_ref, gated_ref):
    length = keys_ref.shape[0]
    gate_rows(keys_ref, values_ref, gated_ref, length)
    decay = jnp.exp(-rates_ref[...])

    def body(step, state):
        base = pl.multiple_of(step * ROWS, ROWS)
        for row in range(ROWS):
            state = decay * state + gated_ref[pl.ds(base + row, 1), :]
        return state

    out_ref[0] = lax.fori_loop(0, length // ROWS, body, jnp.zeros(decay.shape, jnp.float32))


def span_states(keys, values, rates, spans):
    tokens, channels = keys.shape
    length, modes = tokens // spans, rates.shape[0]
    lanes = min(LANES, channels)
    rows = pl.BlockSpec((length, lanes), lambda c, s: (s, c))
    table = pl.BlockSpec((modes, lanes), lambda c, s: (0, c))
    return pl.pallas_call(
        states_kernel,
        out_shape=jax.ShapeDtypeStruct((spans, modes, channels), jnp.float32),
        grid=(channels // lanes, spans),
        in_specs=[rows, rows, table],
        out_specs=pl.BlockSpec((1, modes, lanes), lambda c, s: (s, 0, c)),
        scratch_shapes=[pltpu.VMEM((length, lanes), jnp.float32)],
        name="span_states",
    )(keys, values, rates)


def fold_rows(parts):
    index = lax.broadcasted_iota(jnp.int32, parts[0].shape, 0)
    for bit in (1, 2, 4):
        low = (index & bit) == 0
        parts = [
            jnp.where(low, first, second)
            + pltpu.roll(jnp.where(low, second, first), 8 - bit, axis=0)
            for first, second in zip(parts[0::2], parts[1::2])
        ]
    return parts[0]


def convolve_kernel(
    first, gaps_ref, queries_ref, keys_ref, values_ref, states_ref, residues_ref, rates_ref,
    out_ref, gated_ref,
):
    length = keys_ref.shape[0]
    span = first + pl.program_id(1)
    gate_rows(keys_ref, values_ref, gated_ref, length)
    rates = rates_ref[...]
    decay = jnp.exp(-rates)
    scaled = residues_ref[...] * jnp.sqrt(2.0 * rates)

    def carry(source, state):
        gap = gaps_ref[span, source]
        reach = jnp.exp(-rates * (length * jnp.maximum(gap, 0)).astype(jnp.float32))
        return state + jnp.where(gap >= 0, reach, 0.0) * states_ref[source]

    entering = lax.fori_loop(0, states_ref.shape[0], carry, jnp.zeros(rates.shape, jnp.float32))

    def body(step, state):
        base = pl.multiple_of(step * ROWS, ROWS)
        groups = []
        for group in range(0, ROWS, 8):
            parts = []
            for row in range(group, group + 8):
                state = decay * state + gated_ref[pl.ds(base + row, 1), :]
                seen = scaled * state
                total = seen[0:8]
                for mode in range(8, seen.shape[0], 8):
                    total = total + seen[mode : mode + 8]
                parts.append(total)
            groups.append(fold_rows(parts))
        mixed = jnp.concatenate(groups, axis=0).astype(jnp.bfloat16).astype(jnp.float32)
        rows = pl.ds(base, ROWS)
        out_ref[rows, :] = (queries_ref[rows, :].astype(jnp.float32) * mixed).astype(jnp.bfloat16)
        return state

    lax.fori_loop(0, length // ROWS, body, entering)


def convolve(queries, keys, values, states, residues, rates, gaps, spans, first, count):
    tokens, channels = keys.shape
    length, modes = tokens // spans, rates.shape[0]
    lanes = min(LANES, channels)
    rows = pl.BlockSpec((length, lanes), lambda c, s, g: (first + s, c))
    table = pl.BlockSpec((modes, lanes), lambda c, s, g: (0, c))
    every = pl.BlockSpec((states.shape[0], modes, lanes), lambda c, s, g: (0, 0, c))
    return pl.pallas_call(
        functools.partial(convolve_kernel, first),
        out_shape=jax.ShapeDtypeStruct((count * length, channels), jnp.bfloat16),
        grid_spec=pltpu.PrefetchScalarGridSpec(
            num_scalar_prefetch=1,
            grid=(channels // lanes, count),
            in_specs=[rows, rows, rows, every, table, table],
            out_specs=pl.BlockSpec((length, lanes), lambda c, s, g: (s, c)),
            scratch_shapes=[pltpu.VMEM((length, lanes), jnp.float32)],
        ),
        name="convolve",
    )(gaps, queries, keys, values, states, residues, rates)


def local(queries, keys, values, residues, rates, out_weight, span_order):
    spans = span_order.shape[0] // lax.axis_size("ctx")
    own = lax.dynamic_slice_in_dim(span_order, lax.axis_index("ctx") * spans, spans)
    gaps = own[:, None] - 1 - span_order[None, :]
    totals = span_states(keys, values, rates, spans)
    half = totals.shape[1] // 2
    states = jnp.concatenate(
        [
            lax.all_gather(totals[:, :half], "ctx", axis=0, tiled=True),
            lax.all_gather(totals[:, half:], "ctx", axis=0, tiled=True),
        ],
        axis=1,
    )
    output = convolve(queries, keys, values, states, residues, rates, gaps, spans, 0, spans)
    partial_value = jnp.dot(output, out_weight, preferred_element_type=jnp.float32).astype(
        jnp.bfloat16
    )
    return lax.psum_scatter(partial_value, "tp", scatter_dimension=1, tiled=True)


def solution(mesh):
    placed = (
        P("ctx", "tp"),
        P("ctx", "tp"),
        P("ctx", "tp"),
        P(None, "tp"),
        P(None, "tp"),
        P("tp", None),
        P(),
    )
    return jax.shard_map(
        local, mesh=mesh, in_specs=placed, out_specs=P("ctx", "tp"), check_vma=False
    )
```

```python
import functools

import jax
import jax.numpy as jnp
from jax import lax
from jax.experimental import pallas as pl
from jax.experimental.pallas import tpu as pltpu
from jax.sharding import PartitionSpec as P


ROWS = 16
LANES = 512
PARTS = 2


def gate_rows(keys_ref, values_ref, gated_ref, length):
    @pl.loop(0, length // 64)
    def _(step):
        rows = pl.ds(pl.multiple_of(step * 64, 64), 64)
        gated = keys_ref[rows, :].astype(jnp.float32) * values_ref[rows, :].astype(jnp.float32)
        gated_ref[rows, :] = gated.astype(jnp.bfloat16).astype(jnp.float32)


def states_kernel(keys_ref, values_ref, rates_ref, out_ref, gated_ref):
    length = keys_ref.shape[0]
    gate_rows(keys_ref, values_ref, gated_ref, length)
    decay = jnp.exp(-rates_ref[...])

    def body(step, state):
        base = pl.multiple_of(step * ROWS, ROWS)
        for row in range(ROWS):
            state = decay * state + gated_ref[pl.ds(base + row, 1), :]
        return state

    out_ref[0] = lax.fori_loop(0, length // ROWS, body, jnp.zeros(decay.shape, jnp.float32))


def span_states(keys, values, rates, spans):
    tokens, channels = keys.shape
    length, modes = tokens // spans, rates.shape[0]
    lanes = min(LANES, channels)
    rows = pl.BlockSpec((length, lanes), lambda c, s: (s, c))
    table = pl.BlockSpec((modes, lanes), lambda c, s: (0, c))
    return pl.pallas_call(
        states_kernel,
        out_shape=jax.ShapeDtypeStruct((spans, modes, channels), jnp.float32),
        grid=(channels // lanes, spans),
        in_specs=[rows, rows, table],
        out_specs=pl.BlockSpec((1, modes, lanes), lambda c, s: (s, 0, c)),
        scratch_shapes=[pltpu.VMEM((length, lanes), jnp.float32)],
        name="span_states",
    )(keys, values, rates)


def fold_rows(parts):
    index = lax.broadcasted_iota(jnp.int32, parts[0].shape, 0)
    for bit in (1, 2, 4):
        low = (index & bit) == 0
        parts = [
            jnp.where(low, first, second)
            + pltpu.roll(jnp.where(low, second, first), 8 - bit, axis=0)
            for first, second in zip(parts[0::2], parts[1::2])
        ]
    return parts[0]


def convolve_kernel(
    first, gaps_ref, queries_ref, keys_ref, values_ref, states_ref, residues_ref, rates_ref,
    out_ref, gated_ref,
):
    length = keys_ref.shape[0]
    span = first + pl.program_id(1)
    gate_rows(keys_ref, values_ref, gated_ref, length)
    rates = rates_ref[...]
    decay = jnp.exp(-rates)
    scaled = residues_ref[...] * jnp.sqrt(2.0 * rates)

    def carry(source, state):
        gap = gaps_ref[span, source]
        reach = jnp.exp(-rates * (length * jnp.maximum(gap, 0)).astype(jnp.float32))
        return state + jnp.where(gap >= 0, reach, 0.0) * states_ref[source]

    entering = lax.fori_loop(0, states_ref.shape[0], carry, jnp.zeros(rates.shape, jnp.float32))

    def body(step, state):
        base = pl.multiple_of(step * ROWS, ROWS)
        groups = []
        for group in range(0, ROWS, 8):
            parts = []
            for row in range(group, group + 8):
                state = decay * state + gated_ref[pl.ds(base + row, 1), :]
                seen = scaled * state
                total = seen[0:8]
                for mode in range(8, seen.shape[0], 8):
                    total = total + seen[mode : mode + 8]
                parts.append(total)
            groups.append(fold_rows(parts))
        mixed = jnp.concatenate(groups, axis=0).astype(jnp.bfloat16).astype(jnp.float32)
        rows = pl.ds(base, ROWS)
        out_ref[rows, :] = (queries_ref[rows, :].astype(jnp.float32) * mixed).astype(jnp.bfloat16)
        return state

    lax.fori_loop(0, length // ROWS, body, entering)


def convolve(queries, keys, values, states, residues, rates, gaps, spans, first, count, part, parts):
    tokens, channels = keys.shape
    length, modes = tokens // spans, rates.shape[0]
    width = channels // parts
    lanes = min(LANES, width)
    start = part * (width // lanes)
    rows = pl.BlockSpec((length, lanes), lambda c, s, g: (first + s, start + c))
    table = pl.BlockSpec((modes, lanes), lambda c, s, g: (0, start + c))
    every = pl.BlockSpec((states.shape[0], modes, lanes), lambda c, s, g: (0, 0, start + c))
    return pl.pallas_call(
        functools.partial(convolve_kernel, first),
        out_shape=jax.ShapeDtypeStruct((count * length, width), jnp.bfloat16),
        grid_spec=pltpu.PrefetchScalarGridSpec(
            num_scalar_prefetch=1,
            grid=(width // lanes, count),
            in_specs=[rows, rows, rows, every, table, table],
            out_specs=pl.BlockSpec((length, lanes), lambda c, s, g: (s, c)),
            scratch_shapes=[pltpu.VMEM((length, lanes), jnp.float32)],
        ),
        name="convolve",
    )(gaps, queries, keys, values, states, residues, rates)


def gather_weights(out_weight, parts):
    n, ctx = lax.axis_size("tp"), lax.axis_size("ctx")
    me, mine = lax.axis_index("tp"), lax.axis_index("ctx")
    channels, columns = out_weight.shape[0], out_weight.shape[1] // n
    rows = channels // ctx
    strip = lax.dynamic_slice_in_dim(out_weight, mine * rows, rows, 0)
    pieces = []
    for shift in range(1, n):
        target = lax.rem(me + shift, n)
        piece = lax.dynamic_slice_in_dim(strip, target * columns, columns, 1)
        pieces.append(lax.ppermute(piece, "tp", [(i, (i + shift) % n) for i in range(n)]))
    held = jnp.stack(pieces)
    bits = ctx.bit_length() - 1
    gathered = []
    for part in range(parts):
        order = list(range(1, bits)) if part % 2 == 0 else list(range(bits - 1, 0, -1))
        order = order + [0]
        width = columns // parts
        block = held[:, :, part * width : (part + 1) * width]
        for bit in order:
            other = lax.ppermute(block, "ctx", [(i, i ^ (1 << bit)) for i in range(ctx)])
            low = ((mine >> bit) & 1) == 0
            block = jnp.stack([jnp.where(low, block, other), jnp.where(low, other, block)])
        lead = [len(order) - 1 - order.index(bit) for bit in range(bits - 1, -1, -1)]
        block = jnp.transpose(block, [bits] + lead + [bits + 1, bits + 2])
        gathered.append(block.reshape(n - 1, channels, width))
    return gathered


def payload_kernel(where_ref, right_ref, left_ref, ahead_ref, behind_ref, to_right_ref, to_left_ref):
    @pl.when(where_ref[2] > 0)
    def _():
        to_right_ref[...] = ahead_ref[...] + right_ref[...]

    @pl.when(where_ref[2] == 0)
    def _():
        to_right_ref[...] = ahead_ref[...]

    @pl.when(where_ref[3] > 0)
    def _():
        to_left_ref[...] = behind_ref[...] + left_ref[...]

    @pl.when(where_ref[3] == 0)
    def _():
        to_left_ref[...] = behind_ref[...]


def payload(where, product, ahead, behind):
    rows, width = ahead.shape
    tile = min(rows, 256)
    moved = pl.BlockSpec((tile, width), lambda i, w: (i, 0))
    return pl.pallas_call(
        payload_kernel,
        out_shape=[jax.ShapeDtypeStruct(ahead.shape, ahead.dtype)] * 2,
        grid_spec=pltpu.PrefetchScalarGridSpec(
            num_scalar_prefetch=1,
            grid=(rows // tile,),
            in_specs=[
                pl.BlockSpec((tile, width), lambda i, w: (i, w[0])),
                pl.BlockSpec((tile, width), lambda i, w: (i, w[1])),
                moved,
                moved,
            ],
            out_specs=[moved, moved],
        ),
        name="payload",
    )(where, product, product, ahead, behind)


def exchange(sent, product, parts):
    n = lax.axis_size("tp")
    me = lax.axis_index("tp")
    rights = [(i, i + 1) for i in range(n - 1)]
    lefts = [(i + 1, i) for i in range(n - 1)]
    ahead, behind = list(sent), list(sent)
    from_left = [[None] * parts for _ in range(n + 1)]
    from_right = [[None] * parts for _ in range(n + 1)]
    for slot in range(1, n + 1):
        for part in range(parts):
            right, left = ahead[part], behind[part]
            if slot > 1:
                step = slot - 1
                where = jnp.stack(
                    [
                        lax.rem(me + n - step, n) * parts + part,
                        lax.rem(me + step, n) * parts + part,
                        (me < step).astype(jnp.int32),
                        (me >= n - step).astype(jnp.int32),
                    ]
                )
                right, left = payload(where, product, right, left)
            right = lax.ppermute(right, "tp", rights)
            left = lax.ppermute(left, "tp", lefts)
            ahead[part], behind[part] = right, left
            from_left[slot][part], from_right[slot][part] = right, left
    gathered = [
        [jnp.where(me >= shift, from_left[shift][part], from_right[n - shift][part]) for part in range(parts)]
        for shift in range(1, n)
    ]
    return gathered, from_left[n], from_right[n]


def local(queries, keys, values, residues, rates, out_weight, span_order):
    n = lax.axis_size("tp")
    me = lax.axis_index("tp")
    parts = PARTS
    spans = span_order.shape[0] // lax.axis_size("ctx")
    own = lax.dynamic_slice_in_dim(span_order, lax.axis_index("ctx") * spans, spans)
    gaps = own[:, None] - 1 - span_order[None, :]
    gather = out_weight.shape[0] // lax.axis_size("ctx") >= 128
    weights = gather_weights(out_weight, parts) if gather else None
    totals = span_states(keys, values, rates, spans)
    half = totals.shape[1] // 2
    states = jnp.concatenate(
        [
            lax.all_gather(totals[:, :half], "ctx", axis=0, tiled=True),
            lax.all_gather(totals[:, half:], "ctx", axis=0, tiled=True),
        ],
        axis=1,
    )
    conv = functools.partial(convolve, queries, keys, values, states, residues, rates, gaps, spans)
    if not gather:
        output = conv(0, spans, 0, 1)
        part = jnp.dot(output, out_weight, preferred_element_type=jnp.float32).astype(jnp.bfloat16)
        return lax.psum_scatter(part, "tp", scatter_dimension=1, tiled=True)
    lower = spans // 2
    sent = []
    for part in range(parts):
        sent.append(conv(0, lower, part, parts))
    rest = conv(lower, spans - lower, 0, 1)
    columns = out_weight.shape[1] // n
    product = jnp.dot(rest, out_weight, preferred_element_type=jnp.float32).astype(jnp.bfloat16)
    gathered, from_left, from_right = exchange(sent, product, parts)
    whole = jnp.concatenate(sent + [piece for pieces in gathered for piece in pieces], axis=1)
    mine = lax.dynamic_slice_in_dim(out_weight, me * columns, columns, 1)
    matrix = jnp.concatenate([mine[None], jnp.concatenate(weights, axis=2)], axis=0)
    matrix = matrix.reshape(n * mine.shape[0], columns)
    upper = jnp.dot(whole, matrix, preferred_element_type=jnp.float32).astype(jnp.bfloat16)
    own_part = lax.dynamic_slice_in_dim(product, me * columns, columns, 1)
    total = (
        own_part.astype(jnp.float32)
        + jnp.concatenate(from_left, axis=1).astype(jnp.float32)
        + jnp.concatenate(from_right, axis=1).astype(jnp.float32)
    )
    return jnp.concatenate([upper, total.astype(jnp.bfloat16)], axis=0)


def solution(mesh):
    placed = (
        P("ctx", "tp"),
        P("ctx", "tp"),
        P("ctx", "tp"),
        P(None, "tp"),
        P(None, "tp"),
        P("tp", None),
        P(),
    )

    return jax.shard_map(local, mesh=mesh, in_specs=placed, out_specs=P("ctx", "tp"), check_vma=False)
```

```python
import functools

import jax
import jax.numpy as jnp
from jax import lax
from jax.experimental import pallas as pl
from jax.experimental.pallas import tpu as pltpu
from jax.sharding import PartitionSpec as P


ROWS = 16
LANES = 512
PARTS = 2
TILE = 128


def gate_rows(keys_ref, values_ref, gated_ref, length):
    @pl.loop(0, length // 64)
    def _(step):
        rows = pl.ds(pl.multiple_of(step * 64, 64), 64)
        gated = keys_ref[rows, :].astype(jnp.float32) * values_ref[rows, :].astype(jnp.float32)
        gated_ref[rows, :] = gated.astype(jnp.bfloat16).astype(jnp.float32)


def states_kernel(keys_ref, values_ref, rates_ref, out_ref, gated_ref):
    length = keys_ref.shape[0]
    gate_rows(keys_ref, values_ref, gated_ref, length)
    decay = jnp.exp(-rates_ref[...])

    def body(step, state):
        base = pl.multiple_of(step * ROWS, ROWS)
        for row in range(ROWS):
            state = decay * state + gated_ref[pl.ds(base + row, 1), :]
        return state

    out_ref[0] = lax.fori_loop(0, length // ROWS, body, jnp.zeros(decay.shape, jnp.float32))


def span_states(keys, values, rates, spans):
    tokens, channels = keys.shape
    length, modes = tokens // spans, rates.shape[0]
    lanes = min(LANES, channels)
    rows = pl.BlockSpec((length, lanes), lambda c, s: (s, c))
    table = pl.BlockSpec((modes, lanes), lambda c, s: (0, c))
    return pl.pallas_call(
        states_kernel,
        out_shape=jax.ShapeDtypeStruct((spans, modes, channels), jnp.float32),
        grid=(channels // lanes, spans),
        in_specs=[rows, rows, table],
        out_specs=pl.BlockSpec((1, modes, lanes), lambda c, s: (s, 0, c)),
        scratch_shapes=[pltpu.VMEM((length, lanes), jnp.float32)],
        compiler_params=pltpu.CompilerParams(vmem_limit_bytes=8 << 20),
        name="span_states",
    )(keys, values, rates)


def fold_rows(parts):
    index = lax.broadcasted_iota(jnp.int32, parts[0].shape, 0)
    for bit in (1, 2, 4):
        low = (index & bit) == 0
        parts = [
            jnp.where(low, first, second)
            + pltpu.roll(jnp.where(low, second, first), 8 - bit, axis=0)
            for first, second in zip(parts[0::2], parts[1::2])
        ]
    return parts[0]


def convolve_kernel(
    span, length, gaps_ref, queries_ref, keys_ref, values_ref, states_ref, residues_ref, rates_ref,
    out_ref, gated_ref,
):
    rows = keys_ref.shape[0]
    gate_rows(keys_ref, values_ref, gated_ref, rows)
    rates = rates_ref[...]
    decay = jnp.exp(-rates)
    scaled = residues_ref[...] * jnp.sqrt(2.0 * rates)

    def carry(source, state):
        gap = gaps_ref[span, source]
        reach = jnp.exp(-rates * (length * jnp.maximum(gap, 0)).astype(jnp.float32))
        return state + jnp.where(gap >= 0, reach, 0.0) * states_ref[source]

    entering = lax.fori_loop(0, states_ref.shape[0], carry, jnp.zeros(rates.shape, jnp.float32))

    def body(step, state):
        base = pl.multiple_of(step * ROWS, ROWS)
        groups = []
        for group in range(0, ROWS, 8):
            parts = []
            for row in range(group, group + 8):
                state = decay * state + gated_ref[pl.ds(base + row, 1), :]
                seen = scaled * state
                total = seen[0:8]
                for mode in range(8, seen.shape[0], 8):
                    total = total + seen[mode : mode + 8]
                parts.append(total)
            groups.append(fold_rows(parts))
        mixed = jnp.concatenate(groups, axis=0).astype(jnp.bfloat16).astype(jnp.float32)
        rows = pl.ds(base, ROWS)
        out_ref[rows, :] = (queries_ref[rows, :].astype(jnp.float32) * mixed).astype(jnp.bfloat16)
        return state

    lax.fori_loop(0, rows // ROWS, body, entering)


def convolve(queries, keys, values, residues, rates, gaps, length, states, span, part, parts):
    channels, modes, rows = keys.shape[1] // parts, rates.shape[0], length
    lanes = min(LANES, channels)
    first = part * (channels // lanes)
    data = pl.BlockSpec((rows, lanes), lambda c, g: (span, first + c))
    table = pl.BlockSpec((modes, lanes), lambda c, g: (0, first + c))
    every = pl.BlockSpec((states.shape[0], modes, lanes), lambda c, g: (0, 0, first + c))
    return pl.pallas_call(
        functools.partial(convolve_kernel, span, length),
        out_shape=jax.ShapeDtypeStruct((rows, channels), jnp.bfloat16),
        grid_spec=pltpu.PrefetchScalarGridSpec(
            num_scalar_prefetch=1,
            grid=(channels // lanes,),
            in_specs=[data, data, data, every, table, table],
            out_specs=pl.BlockSpec((rows, lanes), lambda c, g: (0, c)),
            scratch_shapes=[pltpu.VMEM((rows, lanes), jnp.float32)],
        ),
        compiler_params=pltpu.CompilerParams(vmem_limit_bytes=16 << 20),
        name="convolve",
    )(gaps, queries, keys, values, states, residues, rates)


def gather_weights(out_weight):
    n, ctx = lax.axis_size("tp"), lax.axis_size("ctx")
    me, mine = lax.axis_index("tp"), lax.axis_index("ctx")
    channels, columns = out_weight.shape[0], out_weight.shape[1] // n
    rows = channels // ctx
    strip = lax.dynamic_slice_in_dim(out_weight, mine * rows, rows, 0)
    pieces = []
    for shift in range(1, n):
        target = lax.rem(me + shift, n)
        piece = lax.dynamic_slice_in_dim(strip, target * columns, columns, 1)
        pieces.append(lax.ppermute(piece, "tp", [(i, (i + shift) % n) for i in range(n)]))
    held = jnp.stack(pieces)
    strips = {0: held}
    for other in range(2, ctx, 2):
        strips[other] = lax.ppermute(held, "ctx", [(i, i ^ other) for i in range(ctx)])
    for other in range(0, ctx, 2):
        strips[other + 1] = lax.ppermute(strips[other], "ctx", [(i, i ^ 1) for i in range(ctx)])
    return [strips[other] for other in range(ctx)]


def upper_kernel(n, ctx, parts, where_ref, *refs):
    weight_ref, strips, refs = refs[0], refs[1 : 1 + ctx], refs[1 + ctx :]
    sent, refs = refs[:parts], refs[parts:]
    count = (n - 1) * parts
    lefts, rights, refs = refs[:count], refs[count : 2 * count], refs[2 * count :]
    out_ref, matrix_ref, whole_ref, total_ref, result_ref, weight_sem, strip_sem, sent_sem, moved_sem, out_sem = refs
    columns = matrix_ref.shape[2]
    height = matrix_ref.shape[1] // ctx
    width = sent[0].shape[1]
    me, mine = where_ref[0], where_ref[1]

    own = pltpu.make_async_copy(
        weight_ref.at[:, pl.ds(pl.multiple_of(me * columns, 128), columns)], matrix_ref.at[0], weight_sem
    )
    own.start()
    kept = []
    for part in range(parts):
        copy = pltpu.make_async_copy(sent[part], whole_ref.at[0, :, pl.ds(part * width, width)], sent_sem.at[part])
        copy.start()
        kept.append(copy)
    laid = []
    for shift in range(1, n):
        for part in range(parts):
            at = (shift - 1) * parts + part
            target = whole_ref.at[shift, :, pl.ds(part * width, width)]

            @pl.when(me >= shift)
            def _(at=at, target=target):
                pltpu.make_async_copy(lefts[at], target, moved_sem.at[at]).start()

            @pl.when(me < shift)
            def _(at=at, target=target):
                pltpu.make_async_copy(rights[at], target, moved_sem.at[at]).start()

        for other in range(ctx):
            row = pl.multiple_of(jnp.bitwise_xor(mine, other) * height, 16)
            copy = pltpu.make_async_copy(
                strips[other].at[shift - 1], matrix_ref.at[shift, pl.ds(row, height)], strip_sem.at[shift - 1, other]
            )
            copy.start()
            laid.append(copy)
    for shift in range(n):
        if shift == 0:
            own.wait()
            for copy in kept:
                copy.wait()
        else:
            for part in range(parts):
                at = (shift - 1) * parts + part
                target = whole_ref.at[shift, :, pl.ds(part * width, width)]
                pltpu.make_async_copy(lefts[at], target, moved_sem.at[at]).wait()
            for other in range(ctx):
                laid[(shift - 1) * ctx + other].wait()

        @pl.loop(0, columns // 256)
        def _(step, shift=shift):
            at = pl.ds(pl.multiple_of(step * 256, 256), 256)
            piece = jnp.dot(whole_ref[shift], matrix_ref[shift, :, at], preferred_element_type=jnp.float32)
            if shift == 0:
                total_ref[:, at] = piece
            elif shift < n - 1:
                total_ref[:, at] += piece
            else:
                result_ref[:, at] = (total_ref[:, at] + piece).astype(jnp.bfloat16)

    copy = pltpu.make_async_copy(result_ref, out_ref.at[pl.ds(0, sent[0].shape[0])], out_sem)
    copy.start()
    copy.wait()


def upper(where, out_weight, strips, sent, lefts, rights, rows):
    n, ctx, parts = lax.axis_size("tp"), lax.axis_size("ctx"), len(sent)
    channels, columns = out_weight.shape[0], out_weight.shape[1] // n
    tile = sent[0].shape[0]
    anywhere = pl.BlockSpec(memory_space=pl.ANY)
    operands = [out_weight, *strips, *sent, *lefts, *rights]
    return pl.pallas_call(
        functools.partial(upper_kernel, n, ctx, parts),
        out_shape=jax.ShapeDtypeStruct((rows, columns), jnp.bfloat16),
        grid_spec=pltpu.PrefetchScalarGridSpec(
            num_scalar_prefetch=1,
            grid=(1,),
            in_specs=[anywhere] * len(operands),
            out_specs=anywhere,
            scratch_shapes=[
                pltpu.VMEM((n, channels, columns), jnp.bfloat16),
                pltpu.VMEM((n, tile, channels), jnp.bfloat16),
                pltpu.VMEM((tile, columns), jnp.float32),
                pltpu.VMEM((tile, columns), jnp.bfloat16),
                pltpu.SemaphoreType.DMA(()),
                pltpu.SemaphoreType.DMA((n - 1, ctx)),
                pltpu.SemaphoreType.DMA((parts,)),
                pltpu.SemaphoreType.DMA(((n - 1) * parts,)),
                pltpu.SemaphoreType.DMA(()),
            ],
        ),
        compiler_params=pltpu.CompilerParams(vmem_limit_bytes=24 << 20),
        name="upper",
    )(where, *operands)


def finish_kernel(where_ref, unused_ref, product_ref, left_ref, right_ref, out_ref):
    out_ref[...] = (
        product_ref[...].astype(jnp.float32)
        + left_ref[...].astype(jnp.float32)
        + right_ref[...].astype(jnp.float32)
    ).astype(jnp.bfloat16)


def finish(where, result, product, left, right, part):
    rows, columns = left.shape
    tile, first = min(rows, TILE), result.shape[0] - left.shape[0]
    moved = pl.BlockSpec((tile, columns), lambda i, w: (i, 0))
    return pl.pallas_call(
        finish_kernel,
        out_shape=jax.ShapeDtypeStruct(result.shape, result.dtype),
        grid_spec=pltpu.PrefetchScalarGridSpec(
            num_scalar_prefetch=1,
            grid=(rows // tile,),
            in_specs=[
                pl.BlockSpec(memory_space=pl.ANY),
                pl.BlockSpec((tile, columns), lambda i, w: (i, w[0])),
                moved,
                moved,
            ],
            out_specs=pl.BlockSpec((tile, columns), lambda i, w: (first // tile + i, part)),
        ),
        input_output_aliases={1: 0},
        compiler_params=pltpu.CompilerParams(vmem_limit_bytes=4 << 20),
        name="finish",
    )(where, result, product, left, right)


def payload_kernel(step, where_ref, product_ref, ahead_ref, behind_ref, to_right_ref, to_left_ref):
    width = ahead_ref.shape[1]
    for column, source_ref, target_ref in ((0, ahead_ref, to_right_ref), (1, behind_ref, to_left_ref)):
        at = pl.ds(pl.multiple_of(where_ref[step, column] * width, 128), width)
        adds = where_ref[step, column + 2] > 0

        @pl.when(adds)
        def _(at=at, source_ref=source_ref, target_ref=target_ref):
            @pl.loop(0, source_ref.shape[0] // 64)
            def _(block):
                rows = pl.ds(pl.multiple_of(block * 64, 64), 64)
                target_ref[rows, :] = source_ref[rows, :] + product_ref[rows, at]

        @pl.when(jnp.logical_not(adds))
        def _(source_ref=source_ref, target_ref=target_ref):
            @pl.loop(0, source_ref.shape[0] // 64)
            def _(block):
                rows = pl.ds(pl.multiple_of(block * 64, 64), 64)
                target_ref[rows, :] = source_ref[rows, :]


def payload(where, step, product, ahead, behind):
    inside = pl.BlockSpec(memory_space=pltpu.VMEM)
    return pl.pallas_call(
        functools.partial(payload_kernel, step),
        out_shape=[jax.ShapeDtypeStruct(ahead.shape, ahead.dtype)] * 2,
        in_specs=[pl.BlockSpec(memory_space=pltpu.SMEM), inside, inside, inside],
        out_specs=[inside, inside],
        compiler_params=pltpu.CompilerParams(vmem_limit_bytes=1 << 20),
        name="payload",
    )(where, product, ahead, behind)


def product_kernel(rows_ref, weight_ref, out_ref):
    out_ref[...] = jnp.dot(rows_ref[...], weight_ref[...], preferred_element_type=jnp.float32).astype(jnp.bfloat16)


def local_product(rows, out_weight, part, parts):
    n = lax.axis_size("tp")
    height, channels = rows.shape
    width = out_weight.shape[1] // n // parts
    return pl.pallas_call(
        product_kernel,
        out_shape=jax.ShapeDtypeStruct((height, n * width), jnp.bfloat16),
        grid=(n,),
        in_specs=[
            pl.BlockSpec((height, channels), lambda s: (0, 0)),
            pl.BlockSpec((channels, width), lambda s: (0, s * parts + part)),
        ],
        out_specs=pl.BlockSpec((height, width), lambda s: (0, s)),
        compiler_params=pltpu.CompilerParams(vmem_limit_bytes=16 << 20),
        name="local_product",
    )(rows, out_weight)


def exchange(sent, products):
    n, parts = lax.axis_size("tp"), len(sent)
    me = lax.axis_index("tp")
    rights = [(i, i + 1) for i in range(n - 1)]
    lefts = [(i + 1, i) for i in range(n - 1)]
    ahead, behind = list(sent), list(sent)
    from_left, from_right = {}, {}
    steps = jnp.arange(n)
    table = jnp.stack(
        [
            lax.rem(me + n - steps, n),
            lax.rem(me + steps, n),
            (me < steps).astype(jnp.int32),
            (me >= n - steps).astype(jnp.int32),
        ],
        axis=1,
    )
    for slot in range(1, n + 1):
        for part in range(parts):
            right, left = ahead[part], behind[part]
            if slot > 1:
                right, left = payload(table, slot - 1, products[part], right, left)
            right = lax.ppermute(right, "tp", rights)
            left = lax.ppermute(left, "tp", lefts)
            ahead[part], behind[part] = right, left
            from_left[slot, part], from_right[slot, part] = right, left
    return from_left, from_right


def local(queries, keys, values, residues, rates, out_weight, span_order):
    n, ctx = lax.axis_size("tp"), lax.axis_size("ctx")
    me, mine = lax.axis_index("tp"), lax.axis_index("ctx")
    tokens, channels = queries.shape
    spans = span_order.shape[0] // ctx
    length = tokens // spans
    own = lax.dynamic_slice_in_dim(span_order, mine * spans, spans)
    gaps = own[:, None] - 1 - span_order[None, :]
    lined = channels // ctx >= 128 and spans == 2
    strips = gather_weights(out_weight) if lined else None
    totals = span_states(keys, values, rates, spans)
    half = totals.shape[1] // 2
    states = jnp.concatenate(
        [
            lax.all_gather(totals[:, :half], "ctx", axis=0, tiled=True),
            lax.all_gather(totals[:, half:], "ctx", axis=0, tiled=True),
        ],
        axis=1,
    )
    conv = functools.partial(convolve, queries, keys, values, residues, rates, gaps, length, states)
    if not lined:
        outputs = [conv(span, 0, 1) for span in range(spans)]
        part = jnp.dot(jnp.concatenate(outputs), out_weight, preferred_element_type=jnp.float32)
        return lax.psum_scatter(part.astype(jnp.bfloat16), "tp", scatter_dimension=1, tiled=True)
    sent, products = [], []
    for part in range(PARTS):
        sent.append(conv(0, part, PARTS))
    rest = conv(1, 0, 1)
    for part in range(PARTS):
        products.append(local_product(rest, out_weight, part, PARTS))
    from_left, from_right = exchange(sent, products)
    where = jnp.stack([me, mine])
    lefts = [from_left[shift, part] for shift in range(1, n) for part in range(PARTS)]
    rights = [from_right[n - shift, part] for shift in range(1, n) for part in range(PARTS)]
    result = upper(where, out_weight, strips, sent, lefts, rights, tokens)
    for part in range(PARTS):
        result = finish(
            where, result, products[part], from_left[n, part], from_right[n, part], part
        )
    return result


def solution(mesh):
    placed = (
        P("ctx", "tp"),
        P("ctx", "tp"),
        P("ctx", "tp"),
        P(None, "tp"),
        P(None, "tp"),
        P("tp", None),
        P(),
    )

    return jax.shard_map(local, mesh=mesh, in_specs=placed, out_specs=P("ctx", "tp"), check_vma=False)
```

```python
import functools

import jax
import jax.numpy as jnp
from jax import lax
from jax.experimental import pallas as pl
from jax.experimental.pallas import tpu as pltpu
from jax.sharding import PartitionSpec as P


ROWS = 16
LANES = 512
PARTS = 2


def states_kernel(
    spans, keys_ref, values_ref, rates_ref, out_ref, gated_ref, keys_buf, values_buf, gated_buf, rows_buf, sems
):
    tokens, channels = gated_ref.shape
    length, lanes = tokens // spans, keys_buf.shape[2]
    groups = [(span, first) for first in range(0, channels, lanes) for span in range(spans)]
    copies = []
    for index, (span, first) in enumerate(groups):
        at = (pl.ds(span * length, length), pl.ds(first, lanes))
        pair = [
            pltpu.make_async_copy(keys_ref.at[at], keys_buf.at[index], sems.at[0, index]),
            pltpu.make_async_copy(values_ref.at[at], values_buf.at[index], sems.at[1, index]),
        ]
        for copy in pair:
            copy.start()
        copies.append(pair)
    for index, (span, first) in enumerate(groups):
        for copy in copies[index]:
            copy.wait()
        across = pl.ds(first, lanes)
        decay = jnp.exp(-rates_ref[:, across])

        def body(step, state, index=index, span=span, across=across, decay=decay):
            base = pl.multiple_of(step * ROWS, ROWS)
            rows = pl.ds(base, ROWS)
            keys = keys_buf[index, rows, :].astype(jnp.float32)
            gated = (keys * values_buf[index, rows, :].astype(jnp.float32)).astype(jnp.bfloat16)
            gated_buf[index, rows, :] = gated
            rows_buf[rows, :] = gated.astype(jnp.float32)
            for row in range(ROWS):
                state = decay * state + rows_buf[pl.ds(base + row, 1), :]
            return state

        zero = jnp.zeros(decay.shape, jnp.float32)
        out_ref[span, :, across] = lax.fori_loop(0, length // ROWS, body, zero)
        copy = pltpu.make_async_copy(
            gated_buf.at[index], gated_ref.at[pl.ds(span * length, length), across], sems.at[2, index]
        )
        copy.start()
        copies[index] = copy
    for copy in copies:
        copy.wait()


def span_states(keys, values, rates, spans):
    tokens, channels = keys.shape
    length, modes = tokens // spans, rates.shape[0]
    lanes = min(LANES, channels)
    count = spans * (channels // lanes)
    inside = pl.BlockSpec(memory_space=pltpu.VMEM)
    outside = pl.BlockSpec(memory_space=pltpu.HBM)
    return pl.pallas_call(
        functools.partial(states_kernel, spans),
        out_shape=[
            jax.ShapeDtypeStruct((spans, modes, channels), jnp.float32),
            jax.ShapeDtypeStruct((tokens, channels), jnp.bfloat16),
        ],
        in_specs=[outside, outside, inside],
        out_specs=[inside, outside],
        scratch_shapes=[
            pltpu.VMEM((count, length, lanes), jnp.bfloat16),
            pltpu.VMEM((count, length, lanes), jnp.bfloat16),
            pltpu.VMEM((count, length, lanes), jnp.bfloat16),
            pltpu.VMEM((length, lanes), jnp.float32),
            pltpu.SemaphoreType.DMA((3, count)),
        ],
        compiler_params=pltpu.CompilerParams(vmem_limit_bytes=62 << 20),
        name="span_states",
    )(keys, values, rates)


def fold_rows(parts):
    index = lax.broadcasted_iota(jnp.int32, parts[0].shape, 0)
    for bit in (1, 2, 4):
        low = (index & bit) == 0
        parts = [
            jnp.where(low, first, second)
            + pltpu.roll(jnp.where(low, second, first), 8 - bit, axis=0)
            for first, second in zip(parts[0::2], parts[1::2])
        ]
    return parts[0]


def convolve_kernel(
    span, spans, first, count, order_ref, queries_ref, gated_ref, residues_ref, rates_ref, *refs
):
    states, (out_ref, queries_buf, gated_buf, rows_buf, sems) = refs[:count], refs[count:]
    length, width = out_ref.shape
    lanes = queries_buf.shape[2]
    mine = lax.axis_index("ctx")
    copies = []
    for index in range(width // lanes):
        at = (pl.ds(span * length, length), pl.ds(first + index * lanes, lanes))
        pair = [
            pltpu.make_async_copy(gated_ref.at[at], gated_buf.at[index], sems.at[0, index]),
            pltpu.make_async_copy(queries_ref.at[at], queries_buf.at[index], sems.at[1, index]),
        ]
        for copy in pair:
            copy.start()
        copies.append(pair)
    here = order_ref[mine * spans + span]
    for index in range(width // lanes):
        across = pl.ds(first + index * lanes, lanes)
        rates = rates_ref[:, across]
        decay = jnp.exp(-rates)
        scaled = residues_ref[:, across] * jnp.sqrt(2.0 * rates)
        entering = jnp.zeros(rates.shape, jnp.float32)
        for which, states_ref in enumerate(states):

            def carry(source, state, which=which, states_ref=states_ref, rates=rates, across=across):
                block = source
                if count > 1:
                    other = (source // spans) * count + which
                    block = jnp.bitwise_xor(mine, other) * spans + source % spans
                gap = here - 1 - order_ref[block]
                reach = jnp.exp(-rates * (length * jnp.maximum(gap, 0)).astype(jnp.float32))
                return state + jnp.where(gap >= 0, reach, 0.0) * states_ref[source, :, across]

            entering = lax.fori_loop(0, states_ref.shape[0], carry, entering)
        for copy in copies[index]:
            copy.wait()

        def body(step, state, index=index, decay=decay, scaled=scaled):
            base = pl.multiple_of(step * ROWS, ROWS)
            rows = pl.ds(base, ROWS)
            rows_buf[rows, :] = gated_buf[index, rows, :].astype(jnp.float32)
            groups = []
            for group in range(0, ROWS, 8):
                parts = []
                for row in range(group, group + 8):
                    state = decay * state + rows_buf[pl.ds(base + row, 1), :]
                    seen = scaled * state
                    total = seen[0:8]
                    for mode in range(8, seen.shape[0], 8):
                        total = total + seen[mode : mode + 8]
                    parts.append(total)
                groups.append(fold_rows(parts))
            mixed = jnp.concatenate(groups, axis=0).astype(jnp.bfloat16).astype(jnp.float32)
            gate = queries_buf[index, rows, :].astype(jnp.float32)
            out_ref[rows, index * lanes : (index + 1) * lanes] = (gate * mixed).astype(jnp.bfloat16)
            return state

        lax.fori_loop(0, length // ROWS, body, entering)


def convolve(order, queries, gated, residues, rates, states, spans, span, part, parts):
    tokens, channels = queries.shape
    length, width = tokens // spans, channels // parts
    lanes = min(LANES, width)
    inside = pl.BlockSpec(memory_space=pltpu.VMEM)
    return pl.pallas_call(
        functools.partial(convolve_kernel, span, spans, part * width, len(states)),
        out_shape=jax.ShapeDtypeStruct((length, width), jnp.bfloat16),
        in_specs=[
            pl.BlockSpec(memory_space=pltpu.SMEM),
            pl.BlockSpec(memory_space=pltpu.HBM),
            pl.BlockSpec(memory_space=pltpu.HBM),
            inside,
            inside,
            *[inside] * len(states),
        ],
        out_specs=inside,
        scratch_shapes=[
            pltpu.VMEM((width // lanes, length, lanes), jnp.bfloat16),
            pltpu.VMEM((width // lanes, length, lanes), jnp.bfloat16),
            pltpu.VMEM((length, lanes), jnp.float32),
            pltpu.SemaphoreType.DMA((2, width // lanes)),
        ],
        compiler_params=pltpu.CompilerParams(vmem_limit_bytes=6 << 20),
        name="convolve",
    )(order, queries, gated, residues, rates, *states)


def exchange_states(totals):
    ctx = lax.axis_size("ctx")
    near = [totals]
    for other in range(2, ctx, 2):
        near.append(lax.ppermute(totals, "ctx", [(i, i ^ other) for i in range(ctx)]))
    near = jnp.concatenate(near)
    far = lax.ppermute(near, "ctx", [(i, i ^ 1) for i in range(ctx)])
    return [near, far]


def gather_weights(out_weight):
    n, ctx = lax.axis_size("tp"), lax.axis_size("ctx")
    me, mine = lax.axis_index("tp"), lax.axis_index("ctx")
    channels, columns = out_weight.shape[0], out_weight.shape[1] // n
    rows = channels // ctx
    strip = lax.dynamic_slice_in_dim(out_weight, mine * rows, rows, 0)
    pieces = []
    for shift in range(1, n):
        target = lax.rem(me + shift, n)
        piece = lax.dynamic_slice_in_dim(strip, target * columns, columns, 1)
        pieces.append(lax.ppermute(piece, "tp", [(i, (i + shift) % n) for i in range(n)]))
    held = jnp.stack(pieces)
    strips = {0: held}
    for other in range(2, ctx, 2):
        strips[other] = lax.ppermute(held, "ctx", [(i, i ^ other) for i in range(ctx)])
    for other in range(0, ctx, 2):
        strips[other + 1] = lax.ppermute(strips[other], "ctx", [(i, i ^ 1) for i in range(ctx)])
    return [strips[other] for other in range(ctx)]


def upper_kernel(n, ctx, parts, *refs):
    weight_ref, strips, refs = refs[0], refs[1 : 1 + ctx], refs[1 + ctx :]
    sent, refs = refs[:parts], refs[parts:]
    count = (n - 1) * parts
    evens, odds, refs = refs[:count], refs[count : 2 * count], refs[2 * count :]
    out_ref, matrix_ref, whole_ref, total_ref, result_ref, weight_sem, strip_sem, sent_sem, moved_sem, out_sem = refs
    columns = matrix_ref.shape[2]
    height = matrix_ref.shape[1] // ctx
    width = sent[0].shape[1]
    me, mine = lax.axis_index("tp"), lax.axis_index("ctx")

    own = pltpu.make_async_copy(
        weight_ref.at[:, pl.ds(pl.multiple_of(me * columns, 128), columns)], matrix_ref.at[0], weight_sem
    )
    own.start()
    kept = []
    for part in range(parts):
        copy = pltpu.make_async_copy(sent[part], whole_ref.at[0, :, pl.ds(part * width, width)], sent_sem.at[part])
        copy.start()
        kept.append(copy)
    laid = []
    later = lax.rem(me, 2) == 1
    for shift in range(1, n):
        for part in range(parts):
            at = (shift - 1) * parts + part
            target = whole_ref.at[shift, :, pl.ds(part * width, width)]

            passed = me >= shift
            sources = (
                (passed & later, evens[at]),
                (passed & jnp.logical_not(later), odds[at]),
                (jnp.logical_not(passed) & later, odds[(n - shift - 1) * parts + part]),
                (jnp.logical_not(passed) & jnp.logical_not(later), evens[(n - shift - 1) * parts + part]),
            )
            for taken, source in sources:

                @pl.when(taken)
                def _(at=at, source=source, target=target):
                    pltpu.make_async_copy(source, target, moved_sem.at[at]).start()

        for other in range(ctx):
            row = pl.multiple_of(jnp.bitwise_xor(mine, other) * height, 16)
            copy = pltpu.make_async_copy(
                strips[other].at[shift - 1], matrix_ref.at[shift, pl.ds(row, height)], strip_sem.at[shift - 1, other]
            )
            copy.start()
            laid.append(copy)
    for shift in range(n):
        if shift == 0:
            own.wait()
            for copy in kept:
                copy.wait()
        else:
            for part in range(parts):
                at = (shift - 1) * parts + part
                target = whole_ref.at[shift, :, pl.ds(part * width, width)]
                pltpu.make_async_copy(evens[at], target, moved_sem.at[at]).wait()
            for other in range(ctx):
                laid[(shift - 1) * ctx + other].wait()

        @pl.loop(0, columns // 256)
        def _(step, shift=shift):
            at = pl.ds(pl.multiple_of(step * 256, 256), 256)
            piece = jnp.dot(whole_ref[shift], matrix_ref[shift, :, at], preferred_element_type=jnp.float32)
            if shift == 0:
                total_ref[:, at] = piece
            elif shift < n - 1:
                total_ref[:, at] += piece
            else:
                result_ref[:, at] = (total_ref[:, at] + piece).astype(jnp.bfloat16)

    copy = pltpu.make_async_copy(result_ref, out_ref.at[pl.ds(0, sent[0].shape[0])], out_sem)
    copy.start()
    copy.wait()


def upper(out_weight, strips, sent, evens, odds, rows):
    n, ctx, parts = lax.axis_size("tp"), lax.axis_size("ctx"), len(sent)
    channels, columns = out_weight.shape[0], out_weight.shape[1] // n
    tile = sent[0].shape[0]
    anywhere = pl.BlockSpec(memory_space=pl.ANY)
    operands = [out_weight, *strips, *sent, *evens, *odds]
    return pl.pallas_call(
        functools.partial(upper_kernel, n, ctx, parts),
        out_shape=jax.ShapeDtypeStruct((rows, columns), jnp.bfloat16),
        in_specs=[pl.BlockSpec(memory_space=pltpu.HBM)] + [anywhere] * (len(operands) - 1),
        out_specs=anywhere,
        scratch_shapes=[
            pltpu.VMEM((n, channels, columns), jnp.bfloat16),
            pltpu.VMEM((n, tile, channels), jnp.bfloat16),
            pltpu.VMEM((tile, columns), jnp.float32),
            pltpu.VMEM((tile, columns), jnp.bfloat16),
            pltpu.SemaphoreType.DMA(()),
            pltpu.SemaphoreType.DMA((n - 1, ctx)),
            pltpu.SemaphoreType.DMA((parts,)),
            pltpu.SemaphoreType.DMA(((n - 1) * parts,)),
            pltpu.SemaphoreType.DMA(()),
        ],
        compiler_params=pltpu.CompilerParams(vmem_limit_bytes=24 << 20),
        name="upper",
    )(*operands)


def finish_kernel(part, unused_ref, product_ref, left_ref, right_ref, out_ref, result_ref, sem):
    height, width = left_ref.shape
    at = pl.ds(pl.multiple_of(lax.axis_index("tp") * width, 128), width)

    @pl.loop(0, height // 64)
    def _(block):
        rows = pl.ds(pl.multiple_of(block * 64, 64), 64)
        result_ref[rows, :] = (
            product_ref[rows, at].astype(jnp.float32)
            + left_ref[rows, :].astype(jnp.float32)
            + right_ref[rows, :].astype(jnp.float32)
        ).astype(jnp.bfloat16)

    copy = pltpu.make_async_copy(
        result_ref, out_ref.at[pl.ds(out_ref.shape[0] - height, height), pl.ds(part * width, width)], sem
    )
    copy.start()
    copy.wait()


def finish(result, product, left, right, part):
    inside = pl.BlockSpec(memory_space=pltpu.VMEM)
    anywhere = pl.BlockSpec(memory_space=pl.ANY)
    return pl.pallas_call(
        functools.partial(finish_kernel, part),
        out_shape=jax.ShapeDtypeStruct(result.shape, result.dtype),
        in_specs=[anywhere, inside, inside, inside],
        out_specs=anywhere,
        scratch_shapes=[pltpu.VMEM(left.shape, jnp.bfloat16), pltpu.SemaphoreType.DMA(())],
        input_output_aliases={0: 0},
        compiler_params=pltpu.CompilerParams(vmem_limit_bytes=2 << 20),
        name="finish",
    )(result, product, left, right)


def payload_kernel(n, step, product_ref, even_ref, odd_ref, to_even_ref, to_odd_ref):
    me, width = lax.axis_index("tp"), even_ref.shape[1]
    rightward = (lax.rem(me + n - step, n), (me < step).astype(jnp.int32))
    leftward = (lax.rem(me + step, n), (me >= n - step).astype(jnp.int32))
    first = lax.rem(me, 2) == 0
    for flag, source_ref, target_ref in ((first, odd_ref, to_even_ref), (jnp.logical_not(first), even_ref, to_odd_ref)):
        column = jnp.where(flag, rightward[0], leftward[0])
        adds = jnp.where(flag, rightward[1], leftward[1]) > 0
        at = pl.ds(pl.multiple_of(column * width, 128), width)

        @pl.when(adds)
        def _(at=at, source_ref=source_ref, target_ref=target_ref):
            @pl.loop(0, source_ref.shape[0] // 64)
            def _(block):
                rows = pl.ds(pl.multiple_of(block * 64, 64), 64)
                target_ref[rows, :] = source_ref[rows, :] + product_ref[rows, at]

        @pl.when(jnp.logical_not(adds))
        def _(source_ref=source_ref, target_ref=target_ref):
            @pl.loop(0, source_ref.shape[0] // 64)
            def _(block):
                rows = pl.ds(pl.multiple_of(block * 64, 64), 64)
                target_ref[rows, :] = source_ref[rows, :]


def payload(step, product, even, odd):
    inside = pl.BlockSpec(memory_space=pltpu.VMEM)
    return pl.pallas_call(
        functools.partial(payload_kernel, lax.axis_size("tp"), step),
        out_shape=[jax.ShapeDtypeStruct(even.shape, even.dtype)] * 2,
        in_specs=[inside, inside, inside],
        out_specs=[inside, inside],
        compiler_params=pltpu.CompilerParams(vmem_limit_bytes=1 << 20),
        name="payload",
    )(product, even, odd)


def product_kernel(part, parts, rows_ref, weight_ref, out_ref, weight_buf, sems):
    count, _, width = weight_buf.shape
    copies = []
    for group in range(count):
        copy = pltpu.make_async_copy(
            weight_ref.at[:, pl.ds((group * parts + part) * width, width)], weight_buf.at[group], sems.at[group]
        )
        copy.start()
        copies.append(copy)
    for group in range(count):
        copies[group].wait()
        step = min(width, 256)
        for first in range(0, width, step):
            piece = jnp.dot(
                rows_ref[...], weight_buf[group, :, first : first + step], preferred_element_type=jnp.float32
            )
            out_ref[:, group * width + first : group * width + first + step] = piece.astype(jnp.bfloat16)


def local_product(rows, out_weight, part, parts):
    n = lax.axis_size("tp")
    height, channels = rows.shape
    width = out_weight.shape[1] // n // parts
    inside = pl.BlockSpec(memory_space=pltpu.VMEM)
    return pl.pallas_call(
        functools.partial(product_kernel, part, parts),
        out_shape=jax.ShapeDtypeStruct((height, n * width), jnp.bfloat16),
        in_specs=[inside, pl.BlockSpec(memory_space=pltpu.HBM)],
        out_specs=inside,
        scratch_shapes=[pltpu.VMEM((n, channels, width), jnp.bfloat16), pltpu.SemaphoreType.DMA((n,))],
        compiler_params=pltpu.CompilerParams(vmem_limit_bytes=8 << 20),
        name="local_product",
    )(rows, out_weight)


def exchange(sent, products):
    n, parts = lax.axis_size("tp"), len(sent)
    pairs = [
        [pair for i in range(start, n - 1, 2) for pair in ((i, i + 1), (i + 1, i))] for start in range(2)
    ]
    evens, odds = {}, {}
    for slot in range(1, n + 1):
        for part in range(parts):
            if slot == 1:
                even = odd = sent[part]
            else:
                even, odd = payload(slot - 1, products[part], evens[slot - 1, part], odds[slot - 1, part])
            evens[slot, part] = lax.ppermute(even, "tp", pairs[0])
            odds[slot, part] = lax.ppermute(odd, "tp", pairs[1])
    return evens, odds


def local(queries, keys, values, residues, rates, out_weight, span_order):
    n, ctx = lax.axis_size("tp"), lax.axis_size("ctx")
    tokens, channels = queries.shape
    spans = span_order.shape[0] // ctx
    lined = channels // ctx >= 128 and spans == 2 and ctx & (ctx - 1) == 0
    totals, gated = span_states(keys, values, rates, spans)
    strips = gather_weights(out_weight) if lined else None
    states = exchange_states(totals) if lined else [lax.all_gather(totals, "ctx", axis=0, tiled=True)]
    conv = functools.partial(convolve, span_order, queries, gated, residues, rates, states, spans)
    if not lined:
        outputs = [conv(span, 0, 1) for span in range(spans)]
        part = jnp.dot(jnp.concatenate(outputs), out_weight, preferred_element_type=jnp.float32)
        return lax.psum_scatter(part.astype(jnp.bfloat16), "tp", scatter_dimension=1, tiled=True)
    sent, products = [], []
    for part in range(PARTS):
        sent.append(conv(0, part, PARTS))
    rest = conv(1, 0, 1)
    for part in range(PARTS):
        products.append(local_product(rest, out_weight, part, PARTS))
    evens, odds = exchange(sent, products)
    arrived = [[side[slot, part] for slot in range(1, n) for part in range(PARTS)] for side in (evens, odds)]
    result = upper(out_weight, strips, sent, *arrived, tokens)
    for part in range(PARTS):
        result = finish(result, products[part], evens[n, part], odds[n, part], part)
    return result


def solution(mesh):
    placed = (
        P("ctx", "tp"),
        P("ctx", "tp"),
        P("ctx", "tp"),
        P(None, "tp"),
        P(None, "tp"),
        P("tp", None),
        P(),
    )

    return jax.shard_map(local, mesh=mesh, in_specs=placed, out_specs=P("ctx", "tp"), check_vma=False)
```

```python
import functools

import jax
import jax.numpy as jnp
from jax import lax
from jax.experimental import pallas as pl
from jax.experimental.pallas import tpu as pltpu
from jax.sharding import PartitionSpec as P


ROWS = 16
LANES = 512
PARTS = 2


def held_out(array):
    return pltpu.with_memory_space_constraint(array, pltpu.HBM)


def states_kernel(
    spans, keys_ref, values_ref, rates_hbm, out_ref, gated_ref,
    rates_ref, keys_buf, values_buf, gated_buf, rows_buf, sems, rates_sem,
):
    tokens, channels = gated_ref.shape
    length, lanes = tokens // spans, keys_buf.shape[2]
    groups = [(span, first) for first in range(0, channels, lanes) for span in range(spans)]
    table = pltpu.make_async_copy(rates_hbm, rates_ref, rates_sem)
    table.start()
    copies = []
    for index, (span, first) in enumerate(groups):
        at = (pl.ds(span * length, length), pl.ds(first, lanes))
        pair = [
            pltpu.make_async_copy(keys_ref.at[at], keys_buf.at[index], sems.at[0, index]),
            pltpu.make_async_copy(values_ref.at[at], values_buf.at[index], sems.at[1, index]),
        ]
        for copy in pair:
            copy.start()
        copies.append(pair)
    table.wait()
    for index, (span, first) in enumerate(groups):
        for copy in copies[index]:
            copy.wait()
        across = pl.ds(first, lanes)
        decay = jnp.exp(-rates_ref[:, across])

        def body(step, state, index=index, span=span, across=across, decay=decay):
            base = pl.multiple_of(step * ROWS, ROWS)
            rows = pl.ds(base, ROWS)
            keys = keys_buf[index, rows, :].astype(jnp.float32)
            gated = (keys * values_buf[index, rows, :].astype(jnp.float32)).astype(jnp.bfloat16)
            gated_buf[index, rows, :] = gated
            rows_buf[rows, :] = gated.astype(jnp.float32)
            for row in range(ROWS):
                state = decay * state + rows_buf[pl.ds(base + row, 1), :]
            return state

        zero = jnp.zeros(decay.shape, jnp.float32)
        out_ref[span, :, across] = lax.fori_loop(0, length // ROWS, body, zero)
        copy = pltpu.make_async_copy(
            gated_buf.at[index], gated_ref.at[pl.ds(span * length, length), across], sems.at[2, index]
        )
        copy.start()
        copies[index] = copy
    for copy in copies:
        copy.wait()


def span_states(keys, values, rates, spans):
    tokens, channels = keys.shape
    length, modes = tokens // spans, rates.shape[0]
    lanes = min(LANES, channels)
    count = spans * (channels // lanes)
    inside = pl.BlockSpec(memory_space=pltpu.VMEM)
    outside = pl.BlockSpec(memory_space=pltpu.HBM)
    return pl.pallas_call(
        functools.partial(states_kernel, spans),
        out_shape=[
            jax.ShapeDtypeStruct((spans, modes, channels), jnp.float32),
            jax.ShapeDtypeStruct((tokens, channels), jnp.bfloat16),
        ],
        in_specs=[outside, outside, outside],
        out_specs=[inside, pl.BlockSpec(memory_space=pl.ANY)],
        scratch_shapes=[
            pltpu.VMEM((modes, channels), jnp.float32),
            pltpu.VMEM((count, length, lanes), jnp.bfloat16),
            pltpu.VMEM((count, length, lanes), jnp.bfloat16),
            pltpu.VMEM((count, length, lanes), jnp.bfloat16),
            pltpu.VMEM((length, lanes), jnp.float32),
            pltpu.SemaphoreType.DMA((3, count)),
            pltpu.SemaphoreType.DMA(()),
        ],
        compiler_params=pltpu.CompilerParams(vmem_limit_bytes=8 << 20),
        name="span_states",
    )(held_out(keys), held_out(values), held_out(rates))


def fold_rows(parts):
    index = lax.broadcasted_iota(jnp.int32, parts[0].shape, 0)
    for bit in (1, 2, 4):
        low = (index & bit) == 0
        parts = [
            jnp.where(low, first, second)
            + pltpu.roll(jnp.where(low, second, first), 8 - bit, axis=0)
            for first, second in zip(parts[0::2], parts[1::2])
        ]
    return parts[0]


def convolve_kernel(
    span, spans, first, count, order_ref, queries_ref, gated_ref, residues_ref, rates_ref, *refs
):
    states, (out_ref, queries_buf, gated_buf, rows_buf, sems) = refs[:count], refs[count:]
    length, width = out_ref.shape
    lanes = queries_buf.shape[2]
    mine = lax.axis_index("ctx")
    copies = []
    for index in range(width // lanes):
        at = (pl.ds(span * length, length), pl.ds(first + index * lanes, lanes))
        pair = [
            pltpu.make_async_copy(gated_ref.at[at], gated_buf.at[index], sems.at[0, index]),
            pltpu.make_async_copy(queries_ref.at[at], queries_buf.at[index], sems.at[1, index]),
        ]
        for copy in pair:
            copy.start()
        copies.append(pair)
    here = order_ref[mine * spans + span]
    for index in range(width // lanes):
        across = pl.ds(first + index * lanes, lanes)
        rates = rates_ref[:, across]
        decay = jnp.exp(-rates)
        scaled = residues_ref[:, across] * jnp.sqrt(2.0 * rates)
        entering = jnp.zeros(rates.shape, jnp.float32)
        for which, states_ref in enumerate(states):

            def carry(source, state, which=which, states_ref=states_ref, rates=rates, across=across):
                block = source
                if count > 1:
                    other = (source // spans) * count + which
                    block = jnp.bitwise_xor(mine, other) * spans + source % spans
                gap = here - 1 - order_ref[block]
                reach = jnp.exp(-rates * (length * jnp.maximum(gap, 0)).astype(jnp.float32))
                return state + jnp.where(gap >= 0, reach, 0.0) * states_ref[source, :, across]

            entering = lax.fori_loop(0, states_ref.shape[0], carry, entering)
        for copy in copies[index]:
            copy.wait()

        def body(step, state, index=index, decay=decay, scaled=scaled):
            base = pl.multiple_of(step * ROWS, ROWS)
            rows = pl.ds(base, ROWS)
            rows_buf[rows, :] = gated_buf[index, rows, :].astype(jnp.float32)
            groups = []
            for group in range(0, ROWS, 8):
                parts = []
                for row in range(group, group + 8):
                    state = decay * state + rows_buf[pl.ds(base + row, 1), :]
                    seen = scaled * state
                    total = seen[0:8]
                    for mode in range(8, seen.shape[0], 8):
                        total = total + seen[mode : mode + 8]
                    parts.append(total)
                groups.append(fold_rows(parts))
            mixed = jnp.concatenate(groups, axis=0).astype(jnp.bfloat16).astype(jnp.float32)
            gate = queries_buf[index, rows, :].astype(jnp.float32)
            out_ref[rows, index * lanes : (index + 1) * lanes] = (gate * mixed).astype(jnp.bfloat16)
            return state

        lax.fori_loop(0, length // ROWS, body, entering)


def convolve(order, queries, gated, residues, rates, states, spans, span, part, parts):
    tokens, channels = queries.shape
    length, width = tokens // spans, channels // parts
    lanes = min(LANES, width)
    inside = pl.BlockSpec(memory_space=pltpu.VMEM)
    return pl.pallas_call(
        functools.partial(convolve_kernel, span, spans, part * width, len(states)),
        out_shape=jax.ShapeDtypeStruct((length, width), jnp.bfloat16),
        in_specs=[
            pl.BlockSpec(memory_space=pltpu.SMEM),
            pl.BlockSpec(memory_space=pl.ANY),
            pl.BlockSpec(memory_space=pl.ANY),
            inside,
            inside,
            *[inside] * len(states),
        ],
        out_specs=inside,
        scratch_shapes=[
            pltpu.VMEM((width // lanes, length, lanes), jnp.bfloat16),
            pltpu.VMEM((width // lanes, length, lanes), jnp.bfloat16),
            pltpu.VMEM((length, lanes), jnp.float32),
            pltpu.SemaphoreType.DMA((2, width // lanes)),
        ],
        compiler_params=pltpu.CompilerParams(vmem_limit_bytes=6 << 20),
        name="convolve",
    )(order, queries, gated, residues, rates, *states)


def exchange_states(totals):
    ctx = lax.axis_size("ctx")
    near = [totals]
    for other in range(2, ctx, 2):
        near.append(lax.ppermute(totals, "ctx", [(i, i ^ other) for i in range(ctx)]))
    near = jnp.concatenate(near)
    far = lax.ppermute(near, "ctx", [(i, i ^ 1) for i in range(ctx)])
    return [near, far]


def gather_weights(out_weight):
    n, ctx = lax.axis_size("tp"), lax.axis_size("ctx")
    me, mine = lax.axis_index("tp"), lax.axis_index("ctx")
    channels, columns = out_weight.shape[0], out_weight.shape[1] // n
    rows = channels // ctx
    strip = lax.dynamic_slice_in_dim(out_weight, mine * rows, rows, 0)
    pieces = []
    for shift in range(1, n):
        target = lax.rem(me + shift, n)
        piece = lax.dynamic_slice_in_dim(strip, target * columns, columns, 1)
        pieces.append(lax.ppermute(piece, "tp", [(i, (i + shift) % n) for i in range(n)]))
    held = jnp.stack(pieces)
    strips = {0: held}
    for other in range(ctx - 2, 0, -2):
        strips[other] = lax.ppermute(held, "ctx", [(i, i ^ other) for i in range(ctx)])
    for other in range(0, ctx, 2):
        strips[other + 1] = lax.ppermute(strips[other], "ctx", [(i, i ^ 1) for i in range(ctx)])
    return [strips[other] for other in range(ctx)]


def upper_kernel(n, ctx, parts, *refs):
    weight_ref, strips, refs = refs[0], refs[1 : 1 + ctx], refs[1 + ctx :]
    sent, refs = refs[:parts], refs[parts:]
    count = (n - 1) * parts
    evens, odds, refs = refs[:count], refs[count : 2 * count], refs[2 * count :]
    out_ref, matrix_ref, whole_ref, total_ref, result_ref, weight_sem, strip_sem, sent_sem, moved_sem, out_sem = refs
    columns = matrix_ref.shape[2]
    height = matrix_ref.shape[1] // ctx
    width = sent[0].shape[1]
    me, mine = lax.axis_index("tp"), lax.axis_index("ctx")

    own = pltpu.make_async_copy(
        weight_ref.at[:, pl.ds(pl.multiple_of(me * columns, 128), columns)], matrix_ref.at[0], weight_sem
    )
    own.start()
    kept = []
    for part in range(parts):
        copy = pltpu.make_async_copy(sent[part], whole_ref.at[0, :, pl.ds(part * width, width)], sent_sem.at[part])
        copy.start()
        kept.append(copy)
    laid = []
    later = lax.rem(me, 2) == 1
    for shift in range(1, n):
        for part in range(parts):
            at = (shift - 1) * parts + part
            target = whole_ref.at[shift, :, pl.ds(part * width, width)]

            passed = me >= shift
            sources = (
                (passed & later, evens[at]),
                (passed & jnp.logical_not(later), odds[at]),
                (jnp.logical_not(passed) & later, odds[(n - shift - 1) * parts + part]),
                (jnp.logical_not(passed) & jnp.logical_not(later), evens[(n - shift - 1) * parts + part]),
            )
            for taken, source in sources:

                @pl.when(taken)
                def _(at=at, source=source, target=target):
                    pltpu.make_async_copy(source, target, moved_sem.at[at]).start()

        for other in range(ctx):
            row = pl.multiple_of(jnp.bitwise_xor(mine, other) * height, 16)
            copy = pltpu.make_async_copy(
                strips[other].at[shift - 1], matrix_ref.at[shift, pl.ds(row, height)], strip_sem.at[shift - 1, other]
            )
            copy.start()
            laid.append(copy)
    for shift in range(n):
        if shift == 0:
            own.wait()
            for copy in kept:
                copy.wait()
        else:
            for part in range(parts):
                at = (shift - 1) * parts + part
                target = whole_ref.at[shift, :, pl.ds(part * width, width)]
                pltpu.make_async_copy(evens[at], target, moved_sem.at[at]).wait()
            for other in range(ctx):
                laid[(shift - 1) * ctx + other].wait()

        @pl.loop(0, columns // 256)
        def _(step, shift=shift):
            at = pl.ds(pl.multiple_of(step * 256, 256), 256)
            piece = jnp.dot(whole_ref[shift], matrix_ref[shift, :, at], preferred_element_type=jnp.float32)
            if shift == 0:
                total_ref[:, at] = piece
            elif shift < n - 1:
                total_ref[:, at] += piece
            else:
                result_ref[:, at] = (total_ref[:, at] + piece).astype(jnp.bfloat16)

    copy = pltpu.make_async_copy(result_ref, out_ref.at[pl.ds(0, sent[0].shape[0])], out_sem)
    copy.start()
    copy.wait()


def upper(out_weight, strips, sent, evens, odds, rows):
    n, ctx, parts = lax.axis_size("tp"), lax.axis_size("ctx"), len(sent)
    channels, columns = out_weight.shape[0], out_weight.shape[1] // n
    tile = sent[0].shape[0]
    anywhere = pl.BlockSpec(memory_space=pl.ANY)
    operands = [out_weight, *strips, *sent, *evens, *odds]
    return pl.pallas_call(
        functools.partial(upper_kernel, n, ctx, parts),
        out_shape=jax.ShapeDtypeStruct((rows, columns), jnp.bfloat16),
        in_specs=[pl.BlockSpec(memory_space=pltpu.HBM)] + [anywhere] * (len(operands) - 1),
        out_specs=anywhere,
        scratch_shapes=[
            pltpu.VMEM((n, channels, columns), jnp.bfloat16),
            pltpu.VMEM((n, tile, channels), jnp.bfloat16),
            pltpu.VMEM((tile, columns), jnp.float32),
            pltpu.VMEM((tile, columns), jnp.bfloat16),
            pltpu.SemaphoreType.DMA(()),
            pltpu.SemaphoreType.DMA((n - 1, ctx)),
            pltpu.SemaphoreType.DMA((parts,)),
            pltpu.SemaphoreType.DMA(((n - 1) * parts,)),
            pltpu.SemaphoreType.DMA(()),
        ],
        compiler_params=pltpu.CompilerParams(vmem_limit_bytes=24 << 20),
        name="upper",
    )(held_out(out_weight), *operands[1:])


def finish_kernel(part, unused_ref, product_ref, left_ref, right_ref, out_ref, result_ref, sem):
    height, width = left_ref.shape
    at = pl.ds(pl.multiple_of(lax.axis_index("tp") * width, 128), width)

    @pl.loop(0, height // 64)
    def _(block):
        rows = pl.ds(pl.multiple_of(block * 64, 64), 64)
        result_ref[rows, :] = (
            product_ref[rows, at].astype(jnp.float32)
            + left_ref[rows, :].astype(jnp.float32)
            + right_ref[rows, :].astype(jnp.float32)
        ).astype(jnp.bfloat16)

    copy = pltpu.make_async_copy(
        result_ref, out_ref.at[pl.ds(out_ref.shape[0] - height, height), pl.ds(part * width, width)], sem
    )
    copy.start()
    copy.wait()


def finish(result, product, left, right, part):
    inside = pl.BlockSpec(memory_space=pltpu.VMEM)
    anywhere = pl.BlockSpec(memory_space=pl.ANY)
    return pl.pallas_call(
        functools.partial(finish_kernel, part),
        out_shape=jax.ShapeDtypeStruct(result.shape, result.dtype),
        in_specs=[anywhere, inside, inside, inside],
        out_specs=anywhere,
        scratch_shapes=[pltpu.VMEM(left.shape, jnp.bfloat16), pltpu.SemaphoreType.DMA(())],
        input_output_aliases={0: 0},
        compiler_params=pltpu.CompilerParams(vmem_limit_bytes=2 << 20),
        name="finish",
    )(result, product, left, right)


def payload_kernel(n, step, product_ref, even_ref, odd_ref, to_even_ref, to_odd_ref):
    me, width = lax.axis_index("tp"), even_ref.shape[1]
    rightward = (lax.rem(me + n - step, n), (me < step).astype(jnp.int32))
    leftward = (lax.rem(me + step, n), (me >= n - step).astype(jnp.int32))
    first = lax.rem(me, 2) == 0
    for flag, source_ref, target_ref in ((first, odd_ref, to_even_ref), (jnp.logical_not(first), even_ref, to_odd_ref)):
        column = jnp.where(flag, rightward[0], leftward[0])
        adds = jnp.where(flag, rightward[1], leftward[1]) > 0
        at = pl.ds(pl.multiple_of(column * width, 128), width)

        @pl.when(adds)
        def _(at=at, source_ref=source_ref, target_ref=target_ref):
            @pl.loop(0, source_ref.shape[0] // 64)
            def _(block):
                rows = pl.ds(pl.multiple_of(block * 64, 64), 64)
                target_ref[rows, :] = source_ref[rows, :] + product_ref[rows, at]

        @pl.when(jnp.logical_not(adds))
        def _(source_ref=source_ref, target_ref=target_ref):
            @pl.loop(0, source_ref.shape[0] // 64)
            def _(block):
                rows = pl.ds(pl.multiple_of(block * 64, 64), 64)
                target_ref[rows, :] = source_ref[rows, :]


def payload(step, product, even, odd):
    inside = pl.BlockSpec(memory_space=pltpu.VMEM)
    return pl.pallas_call(
        functools.partial(payload_kernel, lax.axis_size("tp"), step),
        out_shape=[jax.ShapeDtypeStruct(even.shape, even.dtype)] * 2,
        in_specs=[inside, inside, inside],
        out_specs=[inside, inside],
        compiler_params=pltpu.CompilerParams(vmem_limit_bytes=1 << 20),
        name="payload",
    )(product, even, odd)


def product_kernel(part, parts, rows_ref, weight_ref, out_ref, weight_buf, sems):
    count, _, width = weight_buf.shape
    copies = []
    for group in range(count):
        copy = pltpu.make_async_copy(
            weight_ref.at[:, pl.ds((group * parts + part) * width, width)], weight_buf.at[group], sems.at[group]
        )
        copy.start()
        copies.append(copy)
    for group in range(count):
        copies[group].wait()
        step = min(width, 256)
        for first in range(0, width, step):
            piece = jnp.dot(
                rows_ref[...], weight_buf[group, :, first : first + step], preferred_element_type=jnp.float32
            )
            out_ref[:, group * width + first : group * width + first + step] = piece.astype(jnp.bfloat16)


def local_product(rows, out_weight, part, parts):
    n = lax.axis_size("tp")
    height, channels = rows.shape
    width = out_weight.shape[1] // n // parts
    inside = pl.BlockSpec(memory_space=pltpu.VMEM)
    return pl.pallas_call(
        functools.partial(product_kernel, part, parts),
        out_shape=jax.ShapeDtypeStruct((height, n * width), jnp.bfloat16),
        in_specs=[inside, pl.BlockSpec(memory_space=pl.ANY)],
        out_specs=inside,
        scratch_shapes=[pltpu.VMEM((n, channels, width), jnp.bfloat16), pltpu.SemaphoreType.DMA((n,))],
        compiler_params=pltpu.CompilerParams(vmem_limit_bytes=8 << 20),
        name="local_product",
    )(rows, out_weight)


def exchange(sent, products):
    n, parts = lax.axis_size("tp"), len(sent)
    pairs = [
        [pair for i in range(start, n - 1, 2) for pair in ((i, i + 1), (i + 1, i))] for start in range(2)
    ]
    evens, odds = {}, {}
    for slot in range(1, n + 1):
        for part in range(parts):
            if slot == 1:
                even = odd = sent[part]
            else:
                even, odd = payload(slot - 1, products[part], evens[slot - 1, part], odds[slot - 1, part])
            evens[slot, part] = lax.ppermute(even, "tp", pairs[0])
            odds[slot, part] = lax.ppermute(odd, "tp", pairs[1])
    return evens, odds


def local(queries, keys, values, residues, rates, out_weight, span_order):
    n, ctx = lax.axis_size("tp"), lax.axis_size("ctx")
    tokens, channels = queries.shape
    spans = span_order.shape[0] // ctx
    lined = channels // ctx >= 128 and spans == 2 and ctx & (ctx - 1) == 0
    totals, gated = span_states(keys, values, rates, spans)
    strips = gather_weights(out_weight) if lined else None
    states = exchange_states(totals) if lined else [lax.all_gather(totals, "ctx", axis=0, tiled=True)]
    conv = functools.partial(convolve, span_order, queries, gated, residues, rates, states, spans)
    if not lined:
        outputs = [conv(span, 0, 1) for span in range(spans)]
        part = jnp.dot(jnp.concatenate(outputs), out_weight, preferred_element_type=jnp.float32)
        return lax.psum_scatter(part.astype(jnp.bfloat16), "tp", scatter_dimension=1, tiled=True)
    sent, products = [], []
    for part in range(PARTS):
        sent.append(conv(0, part, PARTS))
    rest = conv(1, 0, 1)
    for part in range(PARTS):
        products.append(local_product(rest, out_weight, part, PARTS))
    evens, odds = exchange(sent, products)
    arrived = [[side[slot, part] for slot in range(1, n) for part in range(PARTS)] for side in (evens, odds)]
    result = upper(out_weight, strips, sent, *arrived, tokens)
    for part in range(PARTS):
        result = finish(result, products[part], evens[n, part], odds[n, part], part)
    return result


def solution(mesh):
    placed = (
        P("ctx", "tp"),
        P("ctx", "tp"),
        P("ctx", "tp"),
        P(None, "tp"),
        P(None, "tp"),
        P("tp", None),
        P(),
    )

    return jax.shard_map(local, mesh=mesh, in_specs=placed, out_specs=P("ctx", "tp"), check_vma=False)
```

```python
import functools

import jax
import jax.numpy as jnp
from jax import lax
from jax.experimental import pallas as pl
from jax.experimental.pallas import tpu as pltpu
from jax.sharding import PartitionSpec as P


ROWS = 16
LANES = 512
PARTS = 2
FIRST = 4
WIDE = 512
UNROLL = 8
DEPTH = 2


def held_out(array):
    return pltpu.with_memory_space_constraint(array, pltpu.HBM)


def states_kernel(
    spans, keys_ref, values_ref, rates_hbm, out_ref, gated_ref,
    rates_ref, keys_buf, values_buf, gated_buf, rows_buf, sems, rates_sem,
):
    tokens, channels = gated_ref.shape
    length, lanes = tokens // spans, keys_buf.shape[2]
    groups = [(span, first) for first in range(0, channels, lanes) for span in range(spans)]
    table = pltpu.make_async_copy(rates_hbm, rates_ref, rates_sem)
    table.start()
    copies = []
    for index, (span, first) in enumerate(groups):
        at = (pl.ds(span * length, length), pl.ds(first, lanes))
        pair = [
            pltpu.make_async_copy(keys_ref.at[at], keys_buf.at[index], sems.at[0, index]),
            pltpu.make_async_copy(values_ref.at[at], values_buf.at[index], sems.at[1, index]),
        ]
        for copy in pair:
            copy.start()
        copies.append(pair)
    table.wait()
    for index, (span, first) in enumerate(groups):
        for copy in copies[index]:
            copy.wait()
        across = pl.ds(first, lanes)
        decay = jnp.exp(-rates_ref[:, across])

        def body(step, state, index=index, span=span, across=across, decay=decay):
            base = pl.multiple_of(step * ROWS, ROWS)
            rows = pl.ds(base, ROWS)
            keys = keys_buf[index, rows, :].astype(jnp.float32)
            gated = (keys * values_buf[index, rows, :].astype(jnp.float32)).astype(jnp.bfloat16)
            gated_buf[index, rows, :] = gated
            rows_buf[rows, :] = gated.astype(jnp.float32)
            for row in range(ROWS):
                state = decay * state + rows_buf[pl.ds(base + row, 1), :]
            return state

        zero = jnp.zeros(decay.shape, jnp.float32)
        out_ref[span, :, across] = lax.fori_loop(0, length // ROWS, body, zero, unroll=DEPTH)
        copy = pltpu.make_async_copy(
            gated_buf.at[index], gated_ref.at[pl.ds(span * length, length), across], sems.at[2, index]
        )
        copy.start()
        copies[index] = copy
    for copy in copies:
        copy.wait()


def span_states(keys, values, rates, spans):
    tokens, channels = keys.shape
    length, modes = tokens // spans, rates.shape[0]
    lanes = min(WIDE, channels)
    count = spans * (channels // lanes)
    inside = pl.BlockSpec(memory_space=pltpu.VMEM)
    outside = pl.BlockSpec(memory_space=pltpu.HBM)
    return pl.pallas_call(
        functools.partial(states_kernel, spans),
        out_shape=[
            jax.ShapeDtypeStruct((spans, modes, channels), jnp.float32),
            jax.ShapeDtypeStruct((tokens, channels), jnp.bfloat16),
        ],
        in_specs=[outside, outside, outside],
        out_specs=[inside, pl.BlockSpec(memory_space=pl.ANY)],
        scratch_shapes=[
            pltpu.VMEM((modes, channels), jnp.float32),
            pltpu.VMEM((count, length, lanes), jnp.bfloat16),
            pltpu.VMEM((count, length, lanes), jnp.bfloat16),
            pltpu.VMEM((count, length, lanes), jnp.bfloat16),
            pltpu.VMEM((length, lanes), jnp.float32),
            pltpu.SemaphoreType.DMA((3, count)),
            pltpu.SemaphoreType.DMA(()),
        ],
        compiler_params=pltpu.CompilerParams(vmem_limit_bytes=8 << 20),
        name="span_states",
    )(held_out(keys), held_out(values), held_out(rates))


def fold_rows(parts):
    index = lax.broadcasted_iota(jnp.int32, parts[0].shape, 0)
    for bit in (1, 2, 4):
        low = (index & bit) == 0
        parts = [
            jnp.where(low, first, second)
            + pltpu.roll(jnp.where(low, second, first), 8 - bit, axis=0)
            for first, second in zip(parts[0::2], parts[1::2])
        ]
    return parts[0]


def entering_state(span, spans, length, order_ref, rates, states, across):
    mine, count = lax.axis_index("ctx"), len(states)
    here = order_ref[mine * spans + span]
    entering = jnp.zeros(rates.shape, jnp.float32)
    for which, states_ref in enumerate(states):

        def carry(source, state, which=which, states_ref=states_ref):
            block = source
            if count > 1:
                other = (source // spans) * count + which
                block = jnp.bitwise_xor(mine, other) * spans + source % spans
            gap = here - 1 - order_ref[block]
            reach = jnp.exp(-rates * (length * jnp.maximum(gap, 0)).astype(jnp.float32))
            return state + jnp.where(gap >= 0, reach, 0.0) * states_ref[source, :, across]

        entering = lax.fori_loop(0, states_ref.shape[0], carry, entering, unroll=UNROLL)
    return entering


def filtered_rows(decay, scaled, rows_buf, base, state):
    groups = []
    for group in range(0, ROWS, 8):
        parts = []
        for row in range(group, group + 8):
            state = decay * state + rows_buf[pl.ds(base + row, 1), :]
            seen = scaled * state
            total = seen[0:8]
            for mode in range(8, seen.shape[0], 8):
                total = total + seen[mode : mode + 8]
            parts.append(total)
        groups.append(fold_rows(parts))
    return jnp.concatenate(groups, axis=0), state


def convolve_kernel(
    span, spans, first, count, order_ref, queries_ref, gated_ref, residues_ref, rates_ref, *refs
):
    states, (out_ref, queries_buf, gated_buf, rows_buf, sems) = refs[:count], refs[count:]
    length, width = out_ref.shape
    lanes = queries_buf.shape[2]
    copies = []
    for index in range(width // lanes):
        at = (pl.ds(span * length, length), pl.ds(first + index * lanes, lanes))
        pair = [
            pltpu.make_async_copy(gated_ref.at[at], gated_buf.at[index], sems.at[0, index]),
            pltpu.make_async_copy(queries_ref.at[at], queries_buf.at[index], sems.at[1, index]),
        ]
        for copy in pair:
            copy.start()
        copies.append(pair)
    for index in range(width // lanes):
        across = pl.ds(first + index * lanes, lanes)
        rates = rates_ref[:, across]
        decay = jnp.exp(-rates)
        scaled = residues_ref[:, across] * jnp.sqrt(2.0 * rates)
        entering = entering_state(span, spans, length, order_ref, rates, states, across)
        for copy in copies[index]:
            copy.wait()

        def body(step, state, index=index, decay=decay, scaled=scaled):
            base = pl.multiple_of(step * ROWS, ROWS)
            rows = pl.ds(base, ROWS)
            rows_buf[rows, :] = gated_buf[index, rows, :].astype(jnp.float32)
            sums, state = filtered_rows(decay, scaled, rows_buf, base, state)
            mixed = sums.astype(jnp.bfloat16).astype(jnp.float32)
            gate = queries_buf[index, rows, :].astype(jnp.float32)
            out_ref[rows, index * lanes : (index + 1) * lanes] = (gate * mixed).astype(jnp.bfloat16)
            return state

        lax.fori_loop(0, length // ROWS, body, entering, unroll=DEPTH)


def convolve(order, queries, gated, residues, rates, states, spans, span, first, width):
    tokens, _ = queries.shape
    length = tokens // spans
    lanes = width if width % LANES else LANES
    inside = pl.BlockSpec(memory_space=pltpu.VMEM)
    return pl.pallas_call(
        functools.partial(convolve_kernel, span, spans, first, len(states)),
        out_shape=jax.ShapeDtypeStruct((length, width), jnp.bfloat16),
        in_specs=[
            pl.BlockSpec(memory_space=pltpu.SMEM),
            pl.BlockSpec(memory_space=pl.ANY),
            pl.BlockSpec(memory_space=pl.ANY),
            inside,
            inside,
            *[inside] * len(states),
        ],
        out_specs=inside,
        scratch_shapes=[
            pltpu.VMEM((width // lanes, length, lanes), jnp.bfloat16),
            pltpu.VMEM((width // lanes, length, lanes), jnp.bfloat16),
            pltpu.VMEM((length, lanes), jnp.float32),
            pltpu.SemaphoreType.DMA((2, width // lanes)),
        ],
        compiler_params=pltpu.CompilerParams(vmem_limit_bytes=8 << 20),
        name="convolve",
    )(order, queries, gated, residues, rates, *states)


def response_kernel(span, first, gated_ref, residues_ref, rates_ref, out_ref, gated_buf, rows_buf, sem):
    length, width = out_ref.shape
    at = (pl.ds(span * length, length), pl.ds(first, width))
    copy = pltpu.make_async_copy(gated_ref.at[at], gated_buf, sem)
    copy.start()
    rates = rates_ref[:, at[1]]
    decay = jnp.exp(-rates)
    scaled = residues_ref[:, at[1]] * jnp.sqrt(2.0 * rates)
    copy.wait()

    def body(step, state):
        base = pl.multiple_of(step * ROWS, ROWS)
        rows = pl.ds(base, ROWS)
        rows_buf[rows, :] = gated_buf[rows, :].astype(jnp.float32)
        out_ref[rows, :], state = filtered_rows(decay, scaled, rows_buf, base, state)
        return state

    lax.fori_loop(0, length // ROWS, body, jnp.zeros(rates.shape, jnp.float32), unroll=DEPTH)


def span_response(gated, residues, rates, spans, span, first, width):
    length = gated.shape[0] // spans
    inside = pl.BlockSpec(memory_space=pltpu.VMEM)
    return pl.pallas_call(
        functools.partial(response_kernel, span, first),
        out_shape=jax.ShapeDtypeStruct((length, width), jnp.float32),
        in_specs=[pl.BlockSpec(memory_space=pl.ANY), inside, inside],
        out_specs=inside,
        scratch_shapes=[
            pltpu.VMEM((length, width), jnp.bfloat16),
            pltpu.VMEM((length, width), jnp.float32),
            pltpu.SemaphoreType.DMA(()),
        ],
        compiler_params=pltpu.CompilerParams(vmem_limit_bytes=4 << 20),
        name="span_response",
    )(gated, residues, rates)


def complete_kernel(
    span, spans, first, count, order_ref, queries_ref, response_ref, residues_ref, rates_ref, *refs
):
    states, (out_ref, queries_buf, state_buf, sem) = refs[:count], refs[count:]
    length, width = out_ref.shape
    across = pl.ds(first, width)
    copy = pltpu.make_async_copy(queries_ref.at[pl.ds(span * length, length), across], queries_buf, sem)
    copy.start()
    rates = rates_ref[:, across]
    modes = rates.shape[0]
    entering = entering_state(span, spans, length, order_ref, rates, states, across)
    decay = jnp.exp(-rates * float(ROWS))

    def spread(block, state):
        state_buf[block] = state
        return decay * state

    lax.fori_loop(0, length // ROWS, spread, entering, unroll=4)
    copy.wait()
    lags = lax.broadcasted_iota(jnp.int32, (8, 128), 0).astype(jnp.float32)
    for tile in range(0, width, 128):
        here = pl.ds(first + tile, 128)
        cells = slice(tile, tile + 128)
        tables = []
        for mode in range(modes):
            rate = rates_ref[mode : mode + 1, here]
            scale = residues_ref[mode : mode + 1, here] * jnp.sqrt(2.0 * rate)
            tables.append([scale * jnp.exp(-rate * (lags + float(start + 1))) for start in range(0, ROWS, 8)])

        def body(block, unused, tables=tables, cells=cells):
            base = pl.multiple_of(block * ROWS, ROWS)
            sums = []
            for half in range(ROWS // 8):
                total = [response_ref[pl.ds(base + 8 * half, 8), cells], None]
                for mode in range(modes):
                    term = tables[mode][half] * state_buf[block, mode : mode + 1, cells]
                    total[mode % 2] = term if total[mode % 2] is None else total[mode % 2] + term
                sums.append(total[0] + total[1])
            mixed = jnp.concatenate(sums, axis=0).astype(jnp.bfloat16).astype(jnp.float32)
            rows = pl.ds(base, ROWS)
            gate = queries_buf[rows, cells].astype(jnp.float32)
            out_ref[rows, cells] = (gate * mixed).astype(jnp.bfloat16)
            return unused

        lax.fori_loop(0, length // ROWS, body, 0, unroll=2)


def complete(order, queries, response, residues, rates, states, spans, span, first):
    length, width = response.shape
    modes = rates.shape[0]
    inside = pl.BlockSpec(memory_space=pltpu.VMEM)
    return pl.pallas_call(
        functools.partial(complete_kernel, span, spans, first, len(states)),
        out_shape=jax.ShapeDtypeStruct((length, width), jnp.bfloat16),
        in_specs=[
            pl.BlockSpec(memory_space=pltpu.SMEM),
            pl.BlockSpec(memory_space=pl.ANY),
            inside,
            inside,
            inside,
            *[inside] * len(states),
        ],
        out_specs=inside,
        scratch_shapes=[
            pltpu.VMEM((length, width), jnp.bfloat16),
            pltpu.VMEM((length // ROWS, modes, width), jnp.float32),
            pltpu.SemaphoreType.DMA(()),
        ],
        compiler_params=pltpu.CompilerParams(vmem_limit_bytes=4 << 20),
        name="complete",
    )(order, queries, response, residues, rates, *states)


def exchange_states(totals):
    ctx = lax.axis_size("ctx")
    near = [totals]
    for other in range(2, ctx, 2):
        near.append(lax.ppermute(totals, "ctx", [(i, i ^ other) for i in range(ctx)]))
    near = jnp.concatenate(near)
    far = lax.ppermute(near, "ctx", [(i, i ^ 1) for i in range(ctx)])
    return [near, far]


def strips_kernel(weight_ref, *refs):
    outs, sems = refs[:-1], refs[-1]
    rows, columns = outs[0].shape
    start = pl.multiple_of(lax.axis_index("ctx") * rows, 16)
    copies = []
    for index, out_ref in enumerate(outs):
        target = jnp.bitwise_xor(lax.axis_index("tp"), index + 1)
        at = (pl.ds(start, rows), pl.ds(pl.multiple_of(target * columns, 128), columns))
        copy = pltpu.make_async_copy(weight_ref.at[at], out_ref, sems.at[index])
        copy.start()
        copies.append(copy)
    for copy in copies:
        copy.wait()


def weight_strips(out_weight):
    n, ctx = lax.axis_size("tp"), lax.axis_size("ctx")
    shape = (out_weight.shape[0] // ctx, out_weight.shape[1] // n)
    return pl.pallas_call(
        strips_kernel,
        out_shape=[jax.ShapeDtypeStruct(shape, out_weight.dtype)] * (n - 1),
        in_specs=[pl.BlockSpec(memory_space=pl.ANY)],
        out_specs=[pl.BlockSpec(memory_space=pltpu.VMEM)] * (n - 1),
        scratch_shapes=[pltpu.SemaphoreType.DMA((n - 1,))],
        compiler_params=pltpu.CompilerParams(vmem_limit_bytes=1 << 20),
        name="weight_strips",
    )(held_out(out_weight))


def gather_weights(out_weight):
    n, ctx = lax.axis_size("tp"), lax.axis_size("ctx")
    pieces = []
    cut = weight_strips(out_weight)
    for shift in range(1, n):
        pieces.append(lax.ppermute(cut[shift - 1], "tp", [(i, i ^ shift) for i in range(n)]))
    held = jnp.stack(pieces)
    strips = {0: held}
    for other in range(ctx - 2, 0, -2):
        strips[other] = lax.ppermute(held, "ctx", [(i, i ^ other) for i in range(ctx)])
    for other in range(0, ctx, 2):
        strips[other + 1] = lax.ppermute(strips[other], "ctx", [(i, i ^ 1) for i in range(ctx)])
    return [strips[other] for other in range(ctx)]


def upper_kernel(n, ctx, parts, *refs):
    weight_ref, strips, refs = refs[0], refs[1 : 1 + ctx], refs[1 + ctx :]
    sent, refs = refs[:parts], refs[parts:]
    count = (n - 1) * parts
    evens, odds, refs = refs[:count], refs[count : 2 * count], refs[2 * count :]
    out_ref, matrix_ref, whole_ref, total_ref, result_ref, weight_sem, strip_sem, sent_sem, moved_sem, out_sem = refs
    columns = matrix_ref.shape[2]
    height = matrix_ref.shape[1] // ctx
    ends = [sum(ref.shape[1] for ref in sent[:part]) for part in range(parts)]
    spots = [pl.ds(start, ref.shape[1]) for start, ref in zip(ends, sent)]
    me, mine = lax.axis_index("tp"), lax.axis_index("ctx")

    own = pltpu.make_async_copy(
        weight_ref.at[:, pl.ds(pl.multiple_of(me * columns, 128), columns)], matrix_ref.at[0], weight_sem
    )
    own.start()
    kept = []
    for part in range(parts):
        copy = pltpu.make_async_copy(sent[part], whole_ref.at[0, :, spots[part]], sent_sem.at[part])
        copy.start()
        kept.append(copy)
    laid = []
    later = lax.rem(me, 2) == 1
    for shift in range(1, n):
        for part in range(parts):
            at = (shift - 1) * parts + part
            target = whole_ref.at[shift, :, spots[part]]

            away = jnp.bitwise_xor(me, shift) - me
            for slot in range(1, n):
                index = (slot - 1) * parts + part
                for source, sign in ((evens[index], 1), (odds[index], -1)):

                    @pl.when(away == jnp.where(later, -slot * sign, slot * sign))
                    def _(at=at, source=source, target=target):
                        pltpu.make_async_copy(source, target, moved_sem.at[at]).start()

        for other in range(ctx):
            row = pl.multiple_of(jnp.bitwise_xor(mine, other) * height, 16)
            copy = pltpu.make_async_copy(
                strips[other].at[shift - 1], matrix_ref.at[shift, pl.ds(row, height)], strip_sem.at[shift - 1, other]
            )
            copy.start()
            laid.append(copy)
    for shift in range(n):
        if shift == 0:
            own.wait()
            for copy in kept:
                copy.wait()
        else:
            for part in range(parts):
                at = (shift - 1) * parts + part
                target = whole_ref.at[shift, :, spots[part]]
                pltpu.make_async_copy(evens[at], target, moved_sem.at[at]).wait()
            for other in range(ctx):
                laid[(shift - 1) * ctx + other].wait()

        @pl.loop(0, columns // 256)
        def _(step, shift=shift):
            at = pl.ds(pl.multiple_of(step * 256, 256), 256)
            piece = jnp.dot(whole_ref[shift], matrix_ref[shift, :, at], preferred_element_type=jnp.float32)
            if shift == 0:
                total_ref[:, at] = piece
            elif shift < n - 1:
                total_ref[:, at] += piece
            else:
                result_ref[:, at] = (total_ref[:, at] + piece).astype(jnp.bfloat16)

    copy = pltpu.make_async_copy(result_ref, out_ref.at[pl.ds(0, sent[0].shape[0])], out_sem)
    copy.start()
    copy.wait()


def upper(out_weight, strips, sent, evens, odds, rows):
    n, ctx, parts = lax.axis_size("tp"), lax.axis_size("ctx"), len(sent)
    channels, columns = out_weight.shape[0], out_weight.shape[1] // n
    tile = sent[0].shape[0]
    anywhere = pl.BlockSpec(memory_space=pl.ANY)
    operands = [out_weight, *strips, *sent, *evens, *odds]
    return pl.pallas_call(
        functools.partial(upper_kernel, n, ctx, parts),
        out_shape=jax.ShapeDtypeStruct((rows, columns), jnp.bfloat16),
        in_specs=[pl.BlockSpec(memory_space=pltpu.HBM)] + [anywhere] * (len(operands) - 1),
        out_specs=anywhere,
        scratch_shapes=[
            pltpu.VMEM((n, channels, columns), jnp.bfloat16),
            pltpu.VMEM((n, tile, channels), jnp.bfloat16),
            pltpu.VMEM((tile, columns), jnp.float32),
            pltpu.VMEM((tile, columns), jnp.bfloat16),
            pltpu.SemaphoreType.DMA(()),
            pltpu.SemaphoreType.DMA((n - 1, ctx)),
            pltpu.SemaphoreType.DMA((parts,)),
            pltpu.SemaphoreType.DMA(((n - 1) * parts,)),
            pltpu.SemaphoreType.DMA(()),
        ],
        compiler_params=pltpu.CompilerParams(vmem_limit_bytes=24 << 20),
        name="upper",
    )(held_out(out_weight), *operands[1:])


def finish_kernel(first, unused_ref, product_ref, left_ref, right_ref, out_ref, result_ref, sem):
    height, width = left_ref.shape
    at = pl.ds(pl.multiple_of(lax.axis_index("tp") * width, 128), width)

    @pl.loop(0, height // 64)
    def _(block):
        rows = pl.ds(pl.multiple_of(block * 64, 64), 64)
        result_ref[rows, :] = (
            product_ref[rows, at].astype(jnp.float32)
            + left_ref[rows, :].astype(jnp.float32)
            + right_ref[rows, :].astype(jnp.float32)
        ).astype(jnp.bfloat16)

    copy = pltpu.make_async_copy(
        result_ref, out_ref.at[pl.ds(out_ref.shape[0] - height, height), pl.ds(first, width)], sem
    )
    copy.start()
    copy.wait()


def finish(result, product, left, right, first):
    inside = pl.BlockSpec(memory_space=pltpu.VMEM)
    anywhere = pl.BlockSpec(memory_space=pl.ANY)
    return pl.pallas_call(
        functools.partial(finish_kernel, first),
        out_shape=jax.ShapeDtypeStruct(result.shape, result.dtype),
        in_specs=[anywhere, inside, inside, inside],
        out_specs=anywhere,
        scratch_shapes=[pltpu.VMEM(left.shape, jnp.bfloat16), pltpu.SemaphoreType.DMA(())],
        input_output_aliases={0: 0},
        compiler_params=pltpu.CompilerParams(vmem_limit_bytes=2 << 20),
        name="finish",
    )(result, product, left, right)


def payload_kernel(n, step, product_ref, even_ref, odd_ref, to_even_ref, to_odd_ref):
    me, width = lax.axis_index("tp"), even_ref.shape[1]
    rightward = (lax.rem(me + n - step, n), (me < step).astype(jnp.int32))
    leftward = (lax.rem(me + step, n), (me >= n - step).astype(jnp.int32))
    first = lax.rem(me, 2) == 0
    for flag, source_ref, target_ref in ((first, odd_ref, to_even_ref), (jnp.logical_not(first), even_ref, to_odd_ref)):
        column = jnp.where(flag, rightward[0], leftward[0])
        adds = jnp.where(flag, rightward[1], leftward[1]) > 0
        at = pl.ds(pl.multiple_of(column * width, 128), width)

        @pl.when(adds)
        def _(at=at, source_ref=source_ref, target_ref=target_ref):
            @pl.loop(0, source_ref.shape[0] // 64)
            def _(block):
                rows = pl.ds(pl.multiple_of(block * 64, 64), 64)
                target_ref[rows, :] = source_ref[rows, :] + product_ref[rows, at]

        @pl.when(jnp.logical_not(adds))
        def _(source_ref=source_ref, target_ref=target_ref):
            @pl.loop(0, source_ref.shape[0] // 64)
            def _(block):
                rows = pl.ds(pl.multiple_of(block * 64, 64), 64)
                target_ref[rows, :] = source_ref[rows, :]


def payload(step, product, even, odd):
    inside = pl.BlockSpec(memory_space=pltpu.VMEM)
    return pl.pallas_call(
        functools.partial(payload_kernel, lax.axis_size("tp"), step),
        out_shape=[jax.ShapeDtypeStruct(even.shape, even.dtype)] * 2,
        in_specs=[inside, inside, inside],
        out_specs=[inside, inside],
        compiler_params=pltpu.CompilerParams(vmem_limit_bytes=1 << 20),
        name="payload",
    )(product, even, odd)


def product_kernel(start, columns, rows_ref, weight_ref, out_ref, weight_buf, sems):
    count, _, width = weight_buf.shape
    copies = []
    for group in range(count):
        copy = pltpu.make_async_copy(
            weight_ref.at[:, pl.ds(group * columns + start, width)], weight_buf.at[group], sems.at[group]
        )
        copy.start()
        copies.append(copy)
    for group in range(count):
        copies[group].wait()
        for first in range(0, width, 256):
            step = min(width - first, 256)
            piece = jnp.dot(
                rows_ref[...], weight_buf[group, :, first : first + step], preferred_element_type=jnp.float32
            )
            out_ref[:, group * width + first : group * width + first + step] = piece.astype(jnp.bfloat16)


def local_product(rows, out_weight, start, width):
    n = lax.axis_size("tp")
    height, channels = rows.shape
    columns = out_weight.shape[1] // n
    inside = pl.BlockSpec(memory_space=pltpu.VMEM)
    return pl.pallas_call(
        functools.partial(product_kernel, start, columns),
        out_shape=jax.ShapeDtypeStruct((height, n * width), jnp.bfloat16),
        in_specs=[inside, pl.BlockSpec(memory_space=pl.ANY)],
        out_specs=inside,
        scratch_shapes=[pltpu.VMEM((n, channels, width), jnp.bfloat16), pltpu.SemaphoreType.DMA((n,))],
        compiler_params=pltpu.CompilerParams(vmem_limit_bytes=8 << 20),
        name="local_product",
    )(rows, out_weight)


def exchange(sent, products):
    n, parts = lax.axis_size("tp"), len(sent)
    pairs = [
        [pair for i in range(start, n - 1, 2) for pair in ((i, i + 1), (i + 1, i))] for start in range(2)
    ]
    evens, odds = {}, {}
    for slot in range(1, n + 1):
        for part in range(parts):
            if slot == 1:
                even = odd = sent[part]
            else:
                even, odd = payload(slot - 1, products[part], evens[slot - 1, part], odds[slot - 1, part])
            evens[slot, part] = lax.ppermute(even, "tp", pairs[0])
            odds[slot, part] = lax.ppermute(odd, "tp", pairs[1])
    return evens, odds


def local(queries, keys, values, residues, rates, out_weight, span_order):
    n, ctx = lax.axis_size("tp"), lax.axis_size("ctx")
    tokens, channels = queries.shape
    spans = span_order.shape[0] // ctx
    lined = channels // ctx >= 128 and spans == 2 and ctx & (ctx - 1) == 0 and n & (n - 1) == 0
    totals, gated = span_states(keys, values, rates, spans)
    strips = gather_weights(out_weight) if lined else None
    states = exchange_states(totals) if lined else [lax.all_gather(totals, "ctx", axis=0, tiled=True)]
    conv = functools.partial(convolve, span_order, queries, gated, residues, rates, states, spans)
    if not lined:
        outputs = [conv(span, 0, channels) for span in range(spans)]
        part = jnp.dot(jnp.concatenate(outputs), out_weight, preferred_element_type=jnp.float32)
        return lax.psum_scatter(part.astype(jnp.bfloat16), "tp", scatter_dimension=1, tiled=True)
    lead = channels // 128 * FIRST // 8 * 128
    spots = [(0, lead), (lead, channels - lead)]
    sent, products = [], []
    response = span_response(gated, residues, rates, spans, 0, *spots[0])
    sent.append(complete(span_order, queries, response, residues, rates, states, spans, 0, spots[0][0]))
    for part in range(1, PARTS):
        sent.append(conv(0, *spots[part]))
    rest = conv(1, 0, channels)
    for part, spot in enumerate(spots):
        products.append(local_product(rest, out_weight, *spot))
    evens, odds = exchange(sent, products)
    arrived = [[side[slot, part] for slot in range(1, n) for part in range(PARTS)] for side in (evens, odds)]
    result = upper(out_weight, strips, sent, *arrived, tokens)
    for part in range(PARTS):
        result = finish(result, products[part], evens[n, part], odds[n, part], spots[part][0])
    return result


def solution(mesh):
    placed = (
        P("ctx", "tp"),
        P("ctx", "tp"),
        P("ctx", "tp"),
        P(None, "tp"),
        P(None, "tp"),
        P("tp", None),
        P(),
    )

    return jax.shard_map(local, mesh=mesh, in_specs=placed, out_specs=P("ctx", "tp"), check_vma=False)
```

```python
import functools

import jax
import jax.numpy as jnp
from jax import lax
from jax.experimental import pallas as pl
from jax.experimental.pallas import tpu as pltpu
from jax.sharding import PartitionSpec as P


ROWS = 16
LANES = 512
PARTS = 2
FIRST = 4
WIDE = 512
UNROLL = 8
DEPTH = 2


def held_out(array):
    return pltpu.with_memory_space_constraint(array, pltpu.HBM)


def states_kernel(
    spans, keys_ref, values_ref, rates_hbm, out_ref, gated_ref,
    rates_ref, keys_buf, values_buf, gated_buf, rows_buf, sems, rates_sem,
):
    tokens, channels = gated_ref.shape
    length, lanes = tokens // spans, keys_buf.shape[2]
    groups = [(span, first) for first in range(0, channels, lanes) for span in range(spans)]
    table = pltpu.make_async_copy(rates_hbm, rates_ref, rates_sem)
    table.start()
    copies = []
    for index, (span, first) in enumerate(groups):
        at = (pl.ds(span * length, length), pl.ds(first, lanes))
        pair = [
            pltpu.make_async_copy(keys_ref.at[at], keys_buf.at[index], sems.at[0, index]),
            pltpu.make_async_copy(values_ref.at[at], values_buf.at[index], sems.at[1, index]),
        ]
        for copy in pair:
            copy.start()
        copies.append(pair)
    table.wait()
    sent = []
    for start in range(0, len(groups), spans):
        across = pl.ds(groups[start][1], lanes)
        decay = jnp.exp(-rates_ref[:, across])
        for index in range(start, start + spans):
            for copy in copies[index]:
                copy.wait()

        def body(step, states, start=start, decay=decay):
            base = pl.multiple_of(step * ROWS, ROWS)
            rows = pl.ds(base, ROWS)
            for span in range(spans):
                keys = keys_buf[start + span, rows, :].astype(jnp.float32)
                gated = (keys * values_buf[start + span, rows, :].astype(jnp.float32)).astype(jnp.bfloat16)
                gated_buf[start + span, rows, :] = gated
                rows_buf[span, rows, :] = gated.astype(jnp.float32)
            for row in range(ROWS):
                states = tuple(
                    decay * state + rows_buf[span, pl.ds(base + row, 1), :] for span, state in enumerate(states)
                )
            return states

        zeros = tuple(jnp.zeros(decay.shape, jnp.float32) for _ in range(spans))
        finals = lax.fori_loop(0, length // ROWS, body, zeros, unroll=DEPTH)
        for span in range(spans):
            out_ref[span, :, across] = finals[span]
            copy = pltpu.make_async_copy(
                gated_buf.at[start + span],
                gated_ref.at[pl.ds(span * length, length), across],
                sems.at[2, start + span],
            )
            copy.start()
            sent.append(copy)
    for copy in sent:
        copy.wait()


def span_states(keys, values, rates, spans):
    tokens, channels = keys.shape
    length, modes = tokens // spans, rates.shape[0]
    lanes = min(WIDE, channels)
    count = spans * (channels // lanes)
    inside = pl.BlockSpec(memory_space=pltpu.VMEM)
    outside = pl.BlockSpec(memory_space=pltpu.HBM)
    return pl.pallas_call(
        functools.partial(states_kernel, spans),
        out_shape=[
            jax.ShapeDtypeStruct((spans, modes, channels), jnp.float32),
            jax.ShapeDtypeStruct((tokens, channels), jnp.bfloat16),
        ],
        in_specs=[outside, outside, outside],
        out_specs=[inside, pl.BlockSpec(memory_space=pl.ANY)],
        scratch_shapes=[
            pltpu.VMEM((modes, channels), jnp.float32),
            pltpu.VMEM((count, length, lanes), jnp.bfloat16),
            pltpu.VMEM((count, length, lanes), jnp.bfloat16),
            pltpu.VMEM((count, length, lanes), jnp.bfloat16),
            pltpu.VMEM((spans, length, lanes), jnp.float32),
            pltpu.SemaphoreType.DMA((3, count)),
            pltpu.SemaphoreType.DMA(()),
        ],
        compiler_params=pltpu.CompilerParams(vmem_limit_bytes=10 << 20),
        name="span_states",
    )(held_out(keys), held_out(values), held_out(rates))


def fold_rows(parts):
    index = lax.broadcasted_iota(jnp.int32, parts[0].shape, 0)
    for bit in (1, 2, 4):
        low = (index & bit) == 0
        parts = [
            jnp.where(low, first, second)
            + pltpu.roll(jnp.where(low, second, first), 8 - bit, axis=0)
            for first, second in zip(parts[0::2], parts[1::2])
        ]
    return parts[0]


def entering_state(span, spans, length, order_ref, rates, states, across):
    mine, count = lax.axis_index("ctx"), len(states)
    here = order_ref[mine * spans + span]
    entering = jnp.zeros(rates.shape, jnp.float32)
    for which, states_ref in enumerate(states):

        def carry(source, state, which=which, states_ref=states_ref):
            block = source
            if count > 1:
                other = (source // spans) * count + which
                block = jnp.bitwise_xor(mine, other) * spans + source % spans
            gap = here - 1 - order_ref[block]
            reach = jnp.exp(-rates * (length * jnp.maximum(gap, 0)).astype(jnp.float32))
            return state + jnp.where(gap >= 0, reach, 0.0) * states_ref[source, :, across]

        entering = lax.fori_loop(0, states_ref.shape[0], carry, entering, unroll=UNROLL)
    return entering


def filtered_rows(decay, scaled, rows_buf, base, state):
    groups = []
    for group in range(0, ROWS, 8):
        parts = []
        for row in range(group, group + 8):
            state = decay * state + rows_buf[pl.ds(base + row, 1), :]
            seen = scaled * state
            total = seen[0:8]
            for mode in range(8, seen.shape[0], 8):
                total = total + seen[mode : mode + 8]
            parts.append(total)
        groups.append(fold_rows(parts))
    return jnp.concatenate(groups, axis=0), state


def convolve_kernel(
    span, spans, first, count, order_ref, queries_ref, gated_ref, residues_ref, rates_ref, *refs
):
    states, (out_ref, queries_buf, gated_buf, rows_buf, sems) = refs[:count], refs[count:]
    length, width = out_ref.shape
    lanes = queries_buf.shape[2]
    copies = []
    for index in range(width // lanes):
        at = (pl.ds(span * length, length), pl.ds(first + index * lanes, lanes))
        pair = [
            pltpu.make_async_copy(gated_ref.at[at], gated_buf.at[index], sems.at[0, index]),
            pltpu.make_async_copy(queries_ref.at[at], queries_buf.at[index], sems.at[1, index]),
        ]
        for copy in pair:
            copy.start()
        copies.append(pair)
    for index in range(width // lanes):
        across = pl.ds(first + index * lanes, lanes)
        rates = rates_ref[:, across]
        decay = jnp.exp(-rates)
        scaled = residues_ref[:, across] * jnp.sqrt(2.0 * rates)
        entering = entering_state(span, spans, length, order_ref, rates, states, across)
        for copy in copies[index]:
            copy.wait()

        def body(step, state, index=index, decay=decay, scaled=scaled):
            base = pl.multiple_of(step * ROWS, ROWS)
            rows = pl.ds(base, ROWS)
            rows_buf[rows, :] = gated_buf[index, rows, :].astype(jnp.float32)
            sums, state = filtered_rows(decay, scaled, rows_buf, base, state)
            mixed = sums.astype(jnp.bfloat16).astype(jnp.float32)
            gate = queries_buf[index, rows, :].astype(jnp.float32)
            out_ref[rows, index * lanes : (index + 1) * lanes] = (gate * mixed).astype(jnp.bfloat16)
            return state

        lax.fori_loop(0, length // ROWS, body, entering, unroll=DEPTH)


def convolve(order, queries, gated, residues, rates, states, spans, span, first, width):
    tokens, _ = queries.shape
    length = tokens // spans
    lanes = width if width % LANES else LANES
    inside = pl.BlockSpec(memory_space=pltpu.VMEM)
    return pl.pallas_call(
        functools.partial(convolve_kernel, span, spans, first, len(states)),
        out_shape=jax.ShapeDtypeStruct((length, width), jnp.bfloat16),
        in_specs=[
            pl.BlockSpec(memory_space=pltpu.SMEM),
            pl.BlockSpec(memory_space=pl.ANY),
            pl.BlockSpec(memory_space=pl.ANY),
            inside,
            inside,
            *[inside] * len(states),
        ],
        out_specs=inside,
        scratch_shapes=[
            pltpu.VMEM((width // lanes, length, lanes), jnp.bfloat16),
            pltpu.VMEM((width // lanes, length, lanes), jnp.bfloat16),
            pltpu.VMEM((length, lanes), jnp.float32),
            pltpu.SemaphoreType.DMA((2, width // lanes)),
        ],
        compiler_params=pltpu.CompilerParams(vmem_limit_bytes=8 << 20),
        name="convolve",
    )(order, queries, gated, residues, rates, *states)


def response_kernel(span, first, gated_ref, residues_ref, rates_ref, out_ref, gated_buf, rows_buf, sem):
    length, width = out_ref.shape
    at = (pl.ds(span * length, length), pl.ds(first, width))
    copy = pltpu.make_async_copy(gated_ref.at[at], gated_buf, sem)
    copy.start()
    rates = rates_ref[:, at[1]]
    decay = jnp.exp(-rates)
    scaled = residues_ref[:, at[1]] * jnp.sqrt(2.0 * rates)
    copy.wait()

    def body(step, state):
        base = pl.multiple_of(step * ROWS, ROWS)
        rows = pl.ds(base, ROWS)
        rows_buf[rows, :] = gated_buf[rows, :].astype(jnp.float32)
        out_ref[rows, :], state = filtered_rows(decay, scaled, rows_buf, base, state)
        return state

    lax.fori_loop(0, length // ROWS, body, jnp.zeros(rates.shape, jnp.float32), unroll=DEPTH)


def span_response(gated, residues, rates, spans, span, first, width):
    length = gated.shape[0] // spans
    inside = pl.BlockSpec(memory_space=pltpu.VMEM)
    return pl.pallas_call(
        functools.partial(response_kernel, span, first),
        out_shape=jax.ShapeDtypeStruct((length, width), jnp.float32),
        in_specs=[pl.BlockSpec(memory_space=pl.ANY), inside, inside],
        out_specs=inside,
        scratch_shapes=[
            pltpu.VMEM((length, width), jnp.bfloat16),
            pltpu.VMEM((length, width), jnp.float32),
            pltpu.SemaphoreType.DMA(()),
        ],
        compiler_params=pltpu.CompilerParams(vmem_limit_bytes=4 << 20),
        name="span_response",
    )(gated, residues, rates)


def complete_kernel(
    span, spans, first, count, order_ref, queries_ref, response_ref, residues_ref, rates_ref, *refs
):
    states, (out_ref, queries_buf, state_buf, sem) = refs[:count], refs[count:]
    length, width = out_ref.shape
    across = pl.ds(first, width)
    copy = pltpu.make_async_copy(queries_ref.at[pl.ds(span * length, length), across], queries_buf, sem)
    copy.start()
    rates = rates_ref[:, across]
    modes = rates.shape[0]
    entering = entering_state(span, spans, length, order_ref, rates, states, across)
    decay = jnp.exp(-rates * float(ROWS))

    def spread(block, state):
        state_buf[block] = state
        return decay * state

    lax.fori_loop(0, length // ROWS, spread, entering, unroll=4)
    copy.wait()
    lags = lax.broadcasted_iota(jnp.int32, (8, 128), 0).astype(jnp.float32)
    for tile in range(0, width, 128):
        here = pl.ds(first + tile, 128)
        cells = slice(tile, tile + 128)
        tables = []
        for mode in range(modes):
            rate = rates_ref[mode : mode + 1, here]
            scale = residues_ref[mode : mode + 1, here] * jnp.sqrt(2.0 * rate)
            tables.append([scale * jnp.exp(-rate * (lags + float(start + 1))) for start in range(0, ROWS, 8)])

        def body(block, unused, tables=tables, cells=cells):
            base = pl.multiple_of(block * ROWS, ROWS)
            sums = []
            for half in range(ROWS // 8):
                total = [response_ref[pl.ds(base + 8 * half, 8), cells], None]
                for mode in range(modes):
                    term = tables[mode][half] * state_buf[block, mode : mode + 1, cells]
                    total[mode % 2] = term if total[mode % 2] is None else total[mode % 2] + term
                sums.append(total[0] + total[1])
            mixed = jnp.concatenate(sums, axis=0).astype(jnp.bfloat16).astype(jnp.float32)
            rows = pl.ds(base, ROWS)
            gate = queries_buf[rows, cells].astype(jnp.float32)
            out_ref[rows, cells] = (gate * mixed).astype(jnp.bfloat16)
            return unused

        lax.fori_loop(0, length // ROWS, body, 0, unroll=2)


def complete(order, queries, response, residues, rates, states, spans, span, first):
    length, width = response.shape
    modes = rates.shape[0]
    inside = pl.BlockSpec(memory_space=pltpu.VMEM)
    return pl.pallas_call(
        functools.partial(complete_kernel, span, spans, first, len(states)),
        out_shape=jax.ShapeDtypeStruct((length, width), jnp.bfloat16),
        in_specs=[
            pl.BlockSpec(memory_space=pltpu.SMEM),
            pl.BlockSpec(memory_space=pl.ANY),
            inside,
            inside,
            inside,
            *[inside] * len(states),
        ],
        out_specs=inside,
        scratch_shapes=[
            pltpu.VMEM((length, width), jnp.bfloat16),
            pltpu.VMEM((length // ROWS, modes, width), jnp.float32),
            pltpu.SemaphoreType.DMA(()),
        ],
        compiler_params=pltpu.CompilerParams(vmem_limit_bytes=4 << 20),
        name="complete",
    )(order, queries, response, residues, rates, *states)


def exchange_states(totals):
    ctx = lax.axis_size("ctx")
    near = [totals]
    for other in range(2, ctx, 2):
        near.append(lax.ppermute(totals, "ctx", [(i, i ^ other) for i in range(ctx)]))
    near = jnp.concatenate(near)
    far = lax.ppermute(near, "ctx", [(i, i ^ 1) for i in range(ctx)])
    return [near, far]


def strips_kernel(weight_ref, *refs):
    outs, sems = refs[:-1], refs[-1]
    rows, columns = outs[0].shape
    start = pl.multiple_of(lax.axis_index("ctx") * rows, 16)
    copies = []
    for index, out_ref in enumerate(outs):
        target = jnp.bitwise_xor(lax.axis_index("tp"), index + 1)
        at = (pl.ds(start, rows), pl.ds(pl.multiple_of(target * columns, 128), columns))
        copy = pltpu.make_async_copy(weight_ref.at[at], out_ref, sems.at[index])
        copy.start()
        copies.append(copy)
    for copy in copies:
        copy.wait()


def weight_strips(out_weight):
    n, ctx = lax.axis_size("tp"), lax.axis_size("ctx")
    shape = (out_weight.shape[0] // ctx, out_weight.shape[1] // n)
    return pl.pallas_call(
        strips_kernel,
        out_shape=[jax.ShapeDtypeStruct(shape, out_weight.dtype)] * (n - 1),
        in_specs=[pl.BlockSpec(memory_space=pl.ANY)],
        out_specs=[pl.BlockSpec(memory_space=pltpu.VMEM)] * (n - 1),
        scratch_shapes=[pltpu.SemaphoreType.DMA((n - 1,))],
        compiler_params=pltpu.CompilerParams(vmem_limit_bytes=1 << 20),
        name="weight_strips",
    )(held_out(out_weight))


def gather_weights(out_weight):
    n, ctx = lax.axis_size("tp"), lax.axis_size("ctx")
    pieces = []
    cut = weight_strips(out_weight)
    for shift in range(1, n):
        pieces.append(lax.ppermute(cut[shift - 1], "tp", [(i, i ^ shift) for i in range(n)]))
    held = jnp.stack(pieces)
    strips = {0: held}
    for other in range(ctx - 2, 0, -2):
        strips[other] = lax.ppermute(held, "ctx", [(i, i ^ other) for i in range(ctx)])
    for other in range(0, ctx, 2):
        strips[other + 1] = lax.ppermute(strips[other], "ctx", [(i, i ^ 1) for i in range(ctx)])
    return [strips[other] for other in range(ctx)]


def upper_kernel(n, ctx, parts, *refs):
    weight_ref, strips, refs = refs[0], refs[1 : 1 + ctx], refs[1 + ctx :]
    sent, refs = refs[:parts], refs[parts:]
    count = (n - 1) * parts
    evens, odds, refs = refs[:count], refs[count : 2 * count], refs[2 * count :]
    out_ref, matrix_ref, whole_ref, total_ref, result_ref, weight_sem, strip_sem, sent_sem, moved_sem, out_sem = refs
    columns = matrix_ref.shape[2]
    height = matrix_ref.shape[1] // ctx
    ends = [sum(ref.shape[1] for ref in sent[:part]) for part in range(parts)]
    spots = [pl.ds(start, ref.shape[1]) for start, ref in zip(ends, sent)]
    me, mine = lax.axis_index("tp"), lax.axis_index("ctx")

    own = pltpu.make_async_copy(
        weight_ref.at[:, pl.ds(pl.multiple_of(me * columns, 128), columns)], matrix_ref.at[0], weight_sem
    )
    own.start()
    kept = []
    for part in range(parts):
        copy = pltpu.make_async_copy(sent[part], whole_ref.at[0, :, spots[part]], sent_sem.at[part])
        copy.start()
        kept.append(copy)
    laid = []
    later = lax.rem(me, 2) == 1
    for shift in range(1, n):
        for part in range(parts):
            at = (shift - 1) * parts + part
            target = whole_ref.at[shift, :, spots[part]]

            away = jnp.bitwise_xor(me, shift) - me
            for slot in range(1, n):
                index = (slot - 1) * parts + part
                for source, sign in ((evens[index], 1), (odds[index], -1)):

                    @pl.when(away == jnp.where(later, -slot * sign, slot * sign))
                    def _(at=at, source=source, target=target):
                        pltpu.make_async_copy(source, target, moved_sem.at[at]).start()

        for other in range(ctx):
            row = pl.multiple_of(jnp.bitwise_xor(mine, other) * height, 16)
            copy = pltpu.make_async_copy(
                strips[other].at[shift - 1], matrix_ref.at[shift, pl.ds(row, height)], strip_sem.at[shift - 1, other]
            )
            copy.start()
            laid.append(copy)
    for shift in range(n):
        if shift == 0:
            own.wait()
            for copy in kept:
                copy.wait()
        else:
            for part in range(parts):
                at = (shift - 1) * parts + part
                target = whole_ref.at[shift, :, spots[part]]
                pltpu.make_async_copy(evens[at], target, moved_sem.at[at]).wait()
            for other in range(ctx):
                laid[(shift - 1) * ctx + other].wait()

        @pl.loop(0, columns // 256)
        def _(step, shift=shift):
            at = pl.ds(pl.multiple_of(step * 256, 256), 256)
            piece = jnp.dot(whole_ref[shift], matrix_ref[shift, :, at], preferred_element_type=jnp.float32)
            if shift == 0:
                total_ref[:, at] = piece
            elif shift < n - 1:
                total_ref[:, at] += piece
            else:
                result_ref[:, at] = (total_ref[:, at] + piece).astype(jnp.bfloat16)

    copy = pltpu.make_async_copy(result_ref, out_ref.at[pl.ds(0, sent[0].shape[0])], out_sem)
    copy.start()
    copy.wait()


def upper(out_weight, strips, sent, evens, odds, rows):
    n, ctx, parts = lax.axis_size("tp"), lax.axis_size("ctx"), len(sent)
    channels, columns = out_weight.shape[0], out_weight.shape[1] // n
    tile = sent[0].shape[0]
    anywhere = pl.BlockSpec(memory_space=pl.ANY)
    operands = [out_weight, *strips, *sent, *evens, *odds]
    return pl.pallas_call(
        functools.partial(upper_kernel, n, ctx, parts),
        out_shape=jax.ShapeDtypeStruct((rows, columns), jnp.bfloat16),
        in_specs=[pl.BlockSpec(memory_space=pltpu.HBM)] + [anywhere] * (len(operands) - 1),
        out_specs=anywhere,
        scratch_shapes=[
            pltpu.VMEM((n, channels, columns), jnp.bfloat16),
            pltpu.VMEM((n, tile, channels), jnp.bfloat16),
            pltpu.VMEM((tile, columns), jnp.float32),
            pltpu.VMEM((tile, columns), jnp.bfloat16),
            pltpu.SemaphoreType.DMA(()),
            pltpu.SemaphoreType.DMA((n - 1, ctx)),
            pltpu.SemaphoreType.DMA((parts,)),
            pltpu.SemaphoreType.DMA(((n - 1) * parts,)),
            pltpu.SemaphoreType.DMA(()),
        ],
        compiler_params=pltpu.CompilerParams(vmem_limit_bytes=24 << 20),
        name="upper",
    )(held_out(out_weight), *operands[1:])


def finish_kernel(first, unused_ref, product_ref, left_ref, right_ref, out_ref, result_ref, sem):
    height, width = left_ref.shape
    at = pl.ds(pl.multiple_of(lax.axis_index("tp") * width, 128), width)

    @pl.loop(0, height // 64)
    def _(block):
        rows = pl.ds(pl.multiple_of(block * 64, 64), 64)
        result_ref[rows, :] = (
            product_ref[rows, at].astype(jnp.float32)
            + left_ref[rows, :].astype(jnp.float32)
            + right_ref[rows, :].astype(jnp.float32)
        ).astype(jnp.bfloat16)

    copy = pltpu.make_async_copy(
        result_ref, out_ref.at[pl.ds(out_ref.shape[0] - height, height), pl.ds(first, width)], sem
    )
    copy.start()
    copy.wait()


def finish(result, product, left, right, first):
    inside = pl.BlockSpec(memory_space=pltpu.VMEM)
    anywhere = pl.BlockSpec(memory_space=pl.ANY)
    return pl.pallas_call(
        functools.partial(finish_kernel, first),
        out_shape=jax.ShapeDtypeStruct(result.shape, result.dtype),
        in_specs=[anywhere, inside, inside, inside],
        out_specs=anywhere,
        scratch_shapes=[pltpu.VMEM(left.shape, jnp.bfloat16), pltpu.SemaphoreType.DMA(())],
        input_output_aliases={0: 0},
        compiler_params=pltpu.CompilerParams(vmem_limit_bytes=2 << 20),
        name="finish",
    )(result, product, left, right)


def payload_kernel(n, step, product_ref, even_ref, odd_ref, to_even_ref, to_odd_ref):
    me, width = lax.axis_index("tp"), even_ref.shape[1]
    rightward = (lax.rem(me + n - step, n), (me < step).astype(jnp.int32))
    leftward = (lax.rem(me + step, n), (me >= n - step).astype(jnp.int32))
    first = lax.rem(me, 2) == 0
    for flag, source_ref, target_ref in ((first, odd_ref, to_even_ref), (jnp.logical_not(first), even_ref, to_odd_ref)):
        column = jnp.where(flag, rightward[0], leftward[0])
        adds = jnp.where(flag, rightward[1], leftward[1]) > 0
        at = pl.ds(pl.multiple_of(column * width, 128), width)

        @pl.when(adds)
        def _(at=at, source_ref=source_ref, target_ref=target_ref):
            @pl.loop(0, source_ref.shape[0] // 64)
            def _(block):
                rows = pl.ds(pl.multiple_of(block * 64, 64), 64)
                target_ref[rows, :] = source_ref[rows, :] + product_ref[rows, at]

        @pl.when(jnp.logical_not(adds))
        def _(source_ref=source_ref, target_ref=target_ref):
            @pl.loop(0, source_ref.shape[0] // 64)
            def _(block):
                rows = pl.ds(pl.multiple_of(block * 64, 64), 64)
                target_ref[rows, :] = source_ref[rows, :]


def payload(step, product, even, odd):
    inside = pl.BlockSpec(memory_space=pltpu.VMEM)
    return pl.pallas_call(
        functools.partial(payload_kernel, lax.axis_size("tp"), step),
        out_shape=[jax.ShapeDtypeStruct(even.shape, even.dtype)] * 2,
        in_specs=[inside, inside, inside],
        out_specs=[inside, inside],
        compiler_params=pltpu.CompilerParams(vmem_limit_bytes=1 << 20),
        name="payload",
    )(product, even, odd)


def product_kernel(start, columns, rows_ref, weight_ref, out_ref, weight_buf, sems):
    count, _, width = weight_buf.shape
    copies = []
    for group in range(count):
        copy = pltpu.make_async_copy(
            weight_ref.at[:, pl.ds(group * columns + start, width)], weight_buf.at[group], sems.at[group]
        )
        copy.start()
        copies.append(copy)
    for group in range(count):
        copies[group].wait()
        for first in range(0, width, 256):
            step = min(width - first, 256)
            piece = jnp.dot(
                rows_ref[...], weight_buf[group, :, first : first + step], preferred_element_type=jnp.float32
            )
            out_ref[:, group * width + first : group * width + first + step] = piece.astype(jnp.bfloat16)


def local_product(rows, out_weight, start, width):
    n = lax.axis_size("tp")
    height, channels = rows.shape
    columns = out_weight.shape[1] // n
    inside = pl.BlockSpec(memory_space=pltpu.VMEM)
    return pl.pallas_call(
        functools.partial(product_kernel, start, columns),
        out_shape=jax.ShapeDtypeStruct((height, n * width), jnp.bfloat16),
        in_specs=[inside, pl.BlockSpec(memory_space=pl.ANY)],
        out_specs=inside,
        scratch_shapes=[pltpu.VMEM((n, channels, width), jnp.bfloat16), pltpu.SemaphoreType.DMA((n,))],
        compiler_params=pltpu.CompilerParams(vmem_limit_bytes=8 << 20),
        name="local_product",
    )(rows, out_weight)


def exchange(sent, products):
    n, parts = lax.axis_size("tp"), len(sent)
    pairs = [
        [pair for i in range(start, n - 1, 2) for pair in ((i, i + 1), (i + 1, i))] for start in range(2)
    ]
    evens, odds = {}, {}
    for slot in range(1, n + 1):
        for part in range(parts):
            if slot == 1:
                even = odd = sent[part]
            else:
                even, odd = payload(slot - 1, products[part], evens[slot - 1, part], odds[slot - 1, part])
            evens[slot, part] = lax.ppermute(even, "tp", pairs[0])
            odds[slot, part] = lax.ppermute(odd, "tp", pairs[1])
    return evens, odds


def local(queries, keys, values, residues, rates, out_weight, span_order):
    n, ctx = lax.axis_size("tp"), lax.axis_size("ctx")
    tokens, channels = queries.shape
    spans = span_order.shape[0] // ctx
    lined = channels // ctx >= 128 and spans == 2 and ctx & (ctx - 1) == 0 and n & (n - 1) == 0
    totals, gated = span_states(keys, values, rates, spans)
    strips = gather_weights(out_weight) if lined else None
    states = exchange_states(totals) if lined else [lax.all_gather(totals, "ctx", axis=0, tiled=True)]
    conv = functools.partial(convolve, span_order, queries, gated, residues, rates, states, spans)
    if not lined:
        outputs = [conv(span, 0, channels) for span in range(spans)]
        part = jnp.dot(jnp.concatenate(outputs), out_weight, preferred_element_type=jnp.float32)
        return lax.psum_scatter(part.astype(jnp.bfloat16), "tp", scatter_dimension=1, tiled=True)
    lead = channels // 128 * FIRST // 8 * 128
    spots = [(0, lead), (lead, channels - lead)]
    sent, products = [], []
    response = span_response(gated, residues, rates, spans, 0, *spots[0])
    sent.append(complete(span_order, queries, response, residues, rates, states, spans, 0, spots[0][0]))
    for part in range(1, PARTS):
        sent.append(conv(0, *spots[part]))
    rest = conv(1, 0, channels)
    for part, spot in enumerate(spots):
        products.append(local_product(rest, out_weight, *spot))
    evens, odds = exchange(sent, products)
    arrived = [[side[slot, part] for slot in range(1, n) for part in range(PARTS)] for side in (evens, odds)]
    result = upper(out_weight, strips, sent, *arrived, tokens)
    for part in range(PARTS):
        result = finish(result, products[part], evens[n, part], odds[n, part], spots[part][0])
    return result


def solution(mesh):
    placed = (
        P("ctx", "tp"),
        P("ctx", "tp"),
        P("ctx", "tp"),
        P(None, "tp"),
        P(None, "tp"),
        P("tp", None),
        P(),
    )

    return jax.shard_map(local, mesh=mesh, in_specs=placed, out_specs=P("ctx", "tp"), check_vma=False)
```

```python
import functools

import jax
import jax.numpy as jnp
from jax import lax
from jax.experimental import pallas as pl
from jax.experimental.pallas import tpu as pltpu
from jax.sharding import PartitionSpec as P


ROWS = 16
LANES = 512
PARTS = 2
FIRST = 4
WIDE = 512
UNROLL = 8
DEPTH = 4


def held_out(array):
    return pltpu.with_memory_space_constraint(array, pltpu.HBM)


def states_kernel(
    spans, keys_ref, values_ref, rates_hbm, out_ref, gated_ref,
    rates_ref, keys_buf, values_buf, gated_buf, rows_buf, sems, rates_sem,
):
    tokens, channels = gated_ref.shape
    length, lanes = tokens // spans, keys_buf.shape[2]
    groups = [(span, first) for first in range(0, channels, lanes) for span in range(spans)]
    table = pltpu.make_async_copy(rates_hbm, rates_ref, rates_sem)
    table.start()
    copies = []
    for index, (span, first) in enumerate(groups):
        at = (pl.ds(span * length, length), pl.ds(first, lanes))
        pair = [
            pltpu.make_async_copy(keys_ref.at[at], keys_buf.at[index], sems.at[0, index]),
            pltpu.make_async_copy(values_ref.at[at], values_buf.at[index], sems.at[1, index]),
        ]
        for copy in pair:
            copy.start()
        copies.append(pair)
    table.wait()
    sent = []
    for start in range(0, len(groups), spans):
        across = pl.ds(groups[start][1], lanes)
        decay = jnp.exp(-rates_ref[:, across])
        for index in range(start, start + spans):
            for copy in copies[index]:
                copy.wait()

        def body(step, states, start=start, decay=decay):
            base = pl.multiple_of(step * ROWS, ROWS)
            rows = pl.ds(base, ROWS)
            for span in range(spans):
                keys = keys_buf[start + span, rows, :].astype(jnp.float32)
                gated = (keys * values_buf[start + span, rows, :].astype(jnp.float32)).astype(jnp.bfloat16)
                gated_buf[start + span, rows, :] = gated
                rows_buf[span, rows, :] = gated.astype(jnp.float32)
            for row in range(ROWS):
                states = tuple(
                    decay * state + rows_buf[span, pl.ds(base + row, 1), :] for span, state in enumerate(states)
                )
            return states

        zeros = tuple(jnp.zeros(decay.shape, jnp.float32) for _ in range(spans))
        finals = lax.fori_loop(0, length // ROWS, body, zeros, unroll=DEPTH)
        for span in range(spans):
            out_ref[span, :, across] = finals[span]
            copy = pltpu.make_async_copy(
                gated_buf.at[start + span],
                gated_ref.at[pl.ds(span * length, length), across],
                sems.at[2, start + span],
            )
            copy.start()
            sent.append(copy)
    for copy in sent:
        copy.wait()


def span_states(keys, values, rates, spans):
    tokens, channels = keys.shape
    length, modes = tokens // spans, rates.shape[0]
    lanes = min(WIDE, channels)
    count = spans * (channels // lanes)
    inside = pl.BlockSpec(memory_space=pltpu.VMEM)
    outside = pl.BlockSpec(memory_space=pltpu.HBM)
    return pl.pallas_call(
        functools.partial(states_kernel, spans),
        out_shape=[
            jax.ShapeDtypeStruct((spans, modes, channels), jnp.float32),
            jax.ShapeDtypeStruct((tokens, channels), jnp.bfloat16),
        ],
        in_specs=[outside, outside, outside],
        out_specs=[inside, pl.BlockSpec(memory_space=pl.ANY)],
        scratch_shapes=[
            pltpu.VMEM((modes, channels), jnp.float32),
            pltpu.VMEM((count, length, lanes), jnp.bfloat16),
            pltpu.VMEM((count, length, lanes), jnp.bfloat16),
            pltpu.VMEM((count, length, lanes), jnp.bfloat16),
            pltpu.VMEM((spans, length, lanes), jnp.float32),
            pltpu.SemaphoreType.DMA((3, count)),
            pltpu.SemaphoreType.DMA(()),
        ],
        compiler_params=pltpu.CompilerParams(vmem_limit_bytes=10 << 20),
        name="span_states",
    )(held_out(keys), held_out(values), held_out(rates))


def fold_rows(parts):
    index = lax.broadcasted_iota(jnp.int32, parts[0].shape, 0)
    for bit in (1, 2, 4):
        low = (index & bit) == 0
        parts = [
            jnp.where(low, first, second)
            + pltpu.roll(jnp.where(low, second, first), 8 - bit, axis=0)
            for first, second in zip(parts[0::2], parts[1::2])
        ]
    return parts[0]


def entering_state(span, spans, length, order_ref, rates, states, across):
    mine, count = lax.axis_index("ctx"), len(states)
    here = order_ref[mine * spans + span]
    entering = jnp.zeros(rates.shape, jnp.float32)
    for which, states_ref in enumerate(states):

        def carry(source, state, which=which, states_ref=states_ref):
            block = source
            if count > 1:
                other = (source // spans) * count + which
                block = jnp.bitwise_xor(mine, other) * spans + source % spans
            gap = here - 1 - order_ref[block]
            reach = jnp.exp(-rates * (length * jnp.maximum(gap, 0)).astype(jnp.float32))
            return state + jnp.where(gap >= 0, reach, 0.0) * states_ref[source, :, across]

        entering = lax.fori_loop(0, states_ref.shape[0], carry, entering, unroll=UNROLL)
    return entering


def filtered_rows(decay, scaled, rows_buf, base, state):
    groups = []
    for group in range(0, ROWS, 8):
        parts = []
        for row in range(group, group + 8):
            state = decay * state + rows_buf[pl.ds(base + row, 1), :]
            seen = scaled * state
            total = seen[0:8]
            for mode in range(8, seen.shape[0], 8):
                total = total + seen[mode : mode + 8]
            parts.append(total)
        groups.append(fold_rows(parts))
    return jnp.concatenate(groups, axis=0), state


def convolve_kernel(
    span, spans, first, count, order_ref, queries_ref, gated_ref, residues_ref, rates_ref, *refs
):
    states, (out_ref, queries_buf, gated_buf, rows_buf, sems) = refs[:count], refs[count:]
    length, width = out_ref.shape
    lanes = queries_buf.shape[2]
    copies = []
    for index in range(width // lanes):
        at = (pl.ds(span * length, length), pl.ds(first + index * lanes, lanes))
        pair = [
            pltpu.make_async_copy(gated_ref.at[at], gated_buf.at[index], sems.at[0, index]),
            pltpu.make_async_copy(queries_ref.at[at], queries_buf.at[index], sems.at[1, index]),
        ]
        for copy in pair:
            copy.start()
        copies.append(pair)
    for index in range(width // lanes):
        across = pl.ds(first + index * lanes, lanes)
        rates = rates_ref[:, across]
        decay = jnp.exp(-rates)
        scaled = residues_ref[:, across] * jnp.sqrt(2.0 * rates)
        entering = entering_state(span, spans, length, order_ref, rates, states, across)
        for copy in copies[index]:
            copy.wait()

        def body(step, state, index=index, decay=decay, scaled=scaled):
            base = pl.multiple_of(step * ROWS, ROWS)
            rows = pl.ds(base, ROWS)
            rows_buf[rows, :] = gated_buf[index, rows, :].astype(jnp.float32)
            sums, state = filtered_rows(decay, scaled, rows_buf, base, state)
            mixed = sums.astype(jnp.bfloat16).astype(jnp.float32)
            gate = queries_buf[index, rows, :].astype(jnp.float32)
            out_ref[rows, index * lanes : (index + 1) * lanes] = (gate * mixed).astype(jnp.bfloat16)
            return state

        lax.fori_loop(0, length // ROWS, body, entering, unroll=DEPTH)


def convolve(order, queries, gated, residues, rates, states, spans, span, first, width):
    tokens, _ = queries.shape
    length = tokens // spans
    lanes = width if width % LANES else LANES
    inside = pl.BlockSpec(memory_space=pltpu.VMEM)
    return pl.pallas_call(
        functools.partial(convolve_kernel, span, spans, first, len(states)),
        out_shape=jax.ShapeDtypeStruct((length, width), jnp.bfloat16),
        in_specs=[
            pl.BlockSpec(memory_space=pltpu.SMEM),
            pl.BlockSpec(memory_space=pl.ANY),
            pl.BlockSpec(memory_space=pl.ANY),
            inside,
            inside,
            *[inside] * len(states),
        ],
        out_specs=inside,
        scratch_shapes=[
            pltpu.VMEM((width // lanes, length, lanes), jnp.bfloat16),
            pltpu.VMEM((width // lanes, length, lanes), jnp.bfloat16),
            pltpu.VMEM((length, lanes), jnp.float32),
            pltpu.SemaphoreType.DMA((2, width // lanes)),
        ],
        compiler_params=pltpu.CompilerParams(vmem_limit_bytes=8 << 20),
        name="convolve",
    )(order, queries, gated, residues, rates, *states)


def response_kernel(span, first, gated_ref, residues_ref, rates_ref, out_ref, gated_buf, rows_buf, sem):
    length, width = out_ref.shape
    at = (pl.ds(span * length, length), pl.ds(first, width))
    copy = pltpu.make_async_copy(gated_ref.at[at], gated_buf, sem)
    copy.start()
    rates = rates_ref[:, at[1]]
    decay = jnp.exp(-rates)
    scaled = residues_ref[:, at[1]] * jnp.sqrt(2.0 * rates)
    copy.wait()

    def body(step, state):
        base = pl.multiple_of(step * ROWS, ROWS)
        rows = pl.ds(base, ROWS)
        rows_buf[rows, :] = gated_buf[rows, :].astype(jnp.float32)
        out_ref[rows, :], state = filtered_rows(decay, scaled, rows_buf, base, state)
        return state

    lax.fori_loop(0, length // ROWS, body, jnp.zeros(rates.shape, jnp.float32), unroll=DEPTH)


def span_response(gated, residues, rates, spans, span, first, width):
    length = gated.shape[0] // spans
    inside = pl.BlockSpec(memory_space=pltpu.VMEM)
    return pl.pallas_call(
        functools.partial(response_kernel, span, first),
        out_shape=jax.ShapeDtypeStruct((length, width), jnp.float32),
        in_specs=[pl.BlockSpec(memory_space=pl.ANY), inside, inside],
        out_specs=inside,
        scratch_shapes=[
            pltpu.VMEM((length, width), jnp.bfloat16),
            pltpu.VMEM((length, width), jnp.float32),
            pltpu.SemaphoreType.DMA(()),
        ],
        compiler_params=pltpu.CompilerParams(vmem_limit_bytes=4 << 20),
        name="span_response",
    )(gated, residues, rates)


def complete_kernel(
    span, spans, first, count, order_ref, queries_ref, response_ref, residues_ref, rates_ref, *refs
):
    states, (out_ref, queries_buf, state_buf, sem) = refs[:count], refs[count:]
    length, width = out_ref.shape
    across = pl.ds(first, width)
    copy = pltpu.make_async_copy(queries_ref.at[pl.ds(span * length, length), across], queries_buf, sem)
    copy.start()
    rates = rates_ref[:, across]
    modes = rates.shape[0]
    entering = entering_state(span, spans, length, order_ref, rates, states, across)
    decay = jnp.exp(-rates * float(ROWS))

    def spread(block, state):
        state_buf[block] = state
        return decay * state

    lax.fori_loop(0, length // ROWS, spread, entering, unroll=4)
    copy.wait()
    lags = lax.broadcasted_iota(jnp.int32, (8, 128), 0).astype(jnp.float32)
    for tile in range(0, width, 128):
        here = pl.ds(first + tile, 128)
        cells = slice(tile, tile + 128)
        tables = []
        for mode in range(modes):
            rate = rates_ref[mode : mode + 1, here]
            scale = residues_ref[mode : mode + 1, here] * jnp.sqrt(2.0 * rate)
            tables.append([scale * jnp.exp(-rate * (lags + float(start + 1))) for start in range(0, ROWS, 8)])

        def body(block, unused, tables=tables, cells=cells):
            base = pl.multiple_of(block * ROWS, ROWS)
            sums = []
            for half in range(ROWS // 8):
                total = [response_ref[pl.ds(base + 8 * half, 8), cells], None]
                for mode in range(modes):
                    term = tables[mode][half] * state_buf[block, mode : mode + 1, cells]
                    total[mode % 2] = term if total[mode % 2] is None else total[mode % 2] + term
                sums.append(total[0] + total[1])
            mixed = jnp.concatenate(sums, axis=0).astype(jnp.bfloat16).astype(jnp.float32)
            rows = pl.ds(base, ROWS)
            gate = queries_buf[rows, cells].astype(jnp.float32)
            out_ref[rows, cells] = (gate * mixed).astype(jnp.bfloat16)
            return unused

        lax.fori_loop(0, length // ROWS, body, 0, unroll=4)


def complete(order, queries, response, residues, rates, states, spans, span, first):
    length, width = response.shape
    modes = rates.shape[0]
    inside = pl.BlockSpec(memory_space=pltpu.VMEM)
    return pl.pallas_call(
        functools.partial(complete_kernel, span, spans, first, len(states)),
        out_shape=jax.ShapeDtypeStruct((length, width), jnp.bfloat16),
        in_specs=[
            pl.BlockSpec(memory_space=pltpu.SMEM),
            pl.BlockSpec(memory_space=pl.ANY),
            inside,
            inside,
            inside,
            *[inside] * len(states),
        ],
        out_specs=inside,
        scratch_shapes=[
            pltpu.VMEM((length, width), jnp.bfloat16),
            pltpu.VMEM((length // ROWS, modes, width), jnp.float32),
            pltpu.SemaphoreType.DMA(()),
        ],
        compiler_params=pltpu.CompilerParams(vmem_limit_bytes=4 << 20),
        name="complete",
    )(order, queries, response, residues, rates, *states)


def exchange_states(totals):
    ctx = lax.axis_size("ctx")
    near = [totals]
    for other in range(2, ctx, 2):
        near.append(lax.ppermute(totals, "ctx", [(i, i ^ other) for i in range(ctx)]))
    near = jnp.concatenate(near)
    far = lax.ppermute(near, "ctx", [(i, i ^ 1) for i in range(ctx)])
    return [near, far]


def strips_kernel(weight_ref, *refs):
    outs, sems = refs[:-1], refs[-1]
    rows, columns = outs[0].shape
    start = pl.multiple_of(lax.axis_index("ctx") * rows, 16)
    copies = []
    for index, out_ref in enumerate(outs):
        target = jnp.bitwise_xor(lax.axis_index("tp"), index + 1)
        at = (pl.ds(start, rows), pl.ds(pl.multiple_of(target * columns, 128), columns))
        copy = pltpu.make_async_copy(weight_ref.at[at], out_ref, sems.at[index])
        copy.start()
        copies.append(copy)
    for copy in copies:
        copy.wait()


def weight_strips(out_weight):
    n, ctx = lax.axis_size("tp"), lax.axis_size("ctx")
    shape = (out_weight.shape[0] // ctx, out_weight.shape[1] // n)
    return pl.pallas_call(
        strips_kernel,
        out_shape=[jax.ShapeDtypeStruct(shape, out_weight.dtype)] * (n - 1),
        in_specs=[pl.BlockSpec(memory_space=pl.ANY)],
        out_specs=[pl.BlockSpec(memory_space=pltpu.VMEM)] * (n - 1),
        scratch_shapes=[pltpu.SemaphoreType.DMA((n - 1,))],
        compiler_params=pltpu.CompilerParams(vmem_limit_bytes=1 << 20),
        name="weight_strips",
    )(held_out(out_weight))


def gather_weights(out_weight):
    n, ctx = lax.axis_size("tp"), lax.axis_size("ctx")
    pieces = []
    cut = weight_strips(out_weight)
    for shift in range(1, n):
        pieces.append(lax.ppermute(cut[shift - 1], "tp", [(i, i ^ shift) for i in range(n)]))
    held = jnp.stack(pieces)
    strips = {0: held}
    for other in range(ctx - 2, 0, -2):
        strips[other] = lax.ppermute(held, "ctx", [(i, i ^ other) for i in range(ctx)])
    for other in range(0, ctx, 2):
        strips[other + 1] = lax.ppermute(strips[other], "ctx", [(i, i ^ 1) for i in range(ctx)])
    return [strips[other] for other in range(ctx)]


def upper_kernel(n, ctx, parts, *refs):
    weight_ref, strips, refs = refs[0], refs[1 : 1 + ctx], refs[1 + ctx :]
    sent, refs = refs[:parts], refs[parts:]
    count = (n - 1) * parts
    evens, odds, refs = refs[:count], refs[count : 2 * count], refs[2 * count :]
    out_ref, matrix_ref, whole_ref, total_ref, result_ref, weight_sem, strip_sem, sent_sem, moved_sem, out_sem = refs
    columns = matrix_ref.shape[2]
    height = matrix_ref.shape[1] // ctx
    ends = [sum(ref.shape[1] for ref in sent[:part]) for part in range(parts)]
    spots = [pl.ds(start, ref.shape[1]) for start, ref in zip(ends, sent)]
    me, mine = lax.axis_index("tp"), lax.axis_index("ctx")

    own = pltpu.make_async_copy(
        weight_ref.at[:, pl.ds(pl.multiple_of(me * columns, 128), columns)], matrix_ref.at[0], weight_sem
    )
    own.start()
    kept = []
    for part in range(parts):
        copy = pltpu.make_async_copy(sent[part], whole_ref.at[0, :, spots[part]], sent_sem.at[part])
        copy.start()
        kept.append(copy)
    laid = []
    later = lax.rem(me, 2) == 1
    for shift in range(1, n):
        for part in range(parts):
            at = (shift - 1) * parts + part
            target = whole_ref.at[shift, :, spots[part]]

            away = jnp.bitwise_xor(me, shift) - me
            for slot in range(1, n):
                index = (slot - 1) * parts + part
                for source, sign in ((evens[index], 1), (odds[index], -1)):

                    @pl.when(away == jnp.where(later, -slot * sign, slot * sign))
                    def _(at=at, source=source, target=target):
                        pltpu.make_async_copy(source, target, moved_sem.at[at]).start()

        for other in range(ctx):
            row = pl.multiple_of(jnp.bitwise_xor(mine, other) * height, 16)
            copy = pltpu.make_async_copy(
                strips[other].at[shift - 1], matrix_ref.at[shift, pl.ds(row, height)], strip_sem.at[shift - 1, other]
            )
            copy.start()
            laid.append(copy)
    for shift in range(n):
        if shift == 0:
            own.wait()
            for copy in kept:
                copy.wait()
        else:
            for part in range(parts):
                at = (shift - 1) * parts + part
                target = whole_ref.at[shift, :, spots[part]]
                pltpu.make_async_copy(evens[at], target, moved_sem.at[at]).wait()
            for other in range(ctx):
                laid[(shift - 1) * ctx + other].wait()

        @pl.loop(0, columns // 256)
        def _(step, shift=shift):
            at = pl.ds(pl.multiple_of(step * 256, 256), 256)
            piece = jnp.dot(whole_ref[shift], matrix_ref[shift, :, at], preferred_element_type=jnp.float32)
            if shift == 0:
                total_ref[:, at] = piece
            elif shift < n - 1:
                total_ref[:, at] += piece
            else:
                result_ref[:, at] = (total_ref[:, at] + piece).astype(jnp.bfloat16)

    copy = pltpu.make_async_copy(result_ref, out_ref.at[pl.ds(0, sent[0].shape[0])], out_sem)
    copy.start()
    copy.wait()


def upper(out_weight, strips, sent, evens, odds, rows):
    n, ctx, parts = lax.axis_size("tp"), lax.axis_size("ctx"), len(sent)
    channels, columns = out_weight.shape[0], out_weight.shape[1] // n
    tile = sent[0].shape[0]
    anywhere = pl.BlockSpec(memory_space=pl.ANY)
    operands = [out_weight, *strips, *sent, *evens, *odds]
    return pl.pallas_call(
        functools.partial(upper_kernel, n, ctx, parts),
        out_shape=jax.ShapeDtypeStruct((rows, columns), jnp.bfloat16),
        in_specs=[pl.BlockSpec(memory_space=pltpu.HBM)] + [anywhere] * (len(operands) - 1),
        out_specs=anywhere,
        scratch_shapes=[
            pltpu.VMEM((n, channels, columns), jnp.bfloat16),
            pltpu.VMEM((n, tile, channels), jnp.bfloat16),
            pltpu.VMEM((tile, columns), jnp.float32),
            pltpu.VMEM((tile, columns), jnp.bfloat16),
            pltpu.SemaphoreType.DMA(()),
            pltpu.SemaphoreType.DMA((n - 1, ctx)),
            pltpu.SemaphoreType.DMA((parts,)),
            pltpu.SemaphoreType.DMA(((n - 1) * parts,)),
            pltpu.SemaphoreType.DMA(()),
        ],
        compiler_params=pltpu.CompilerParams(vmem_limit_bytes=24 << 20),
        name="upper",
    )(held_out(out_weight), *operands[1:])


def finish_kernel(first, unused_ref, product_ref, left_ref, right_ref, out_ref, result_ref, sem):
    height, width = left_ref.shape
    at = pl.ds(pl.multiple_of(lax.axis_index("tp") * width, 128), width)

    piece = height // 4
    copies = []
    for part in range(4):
        for start in range(part * piece, (part + 1) * piece, 64):
            rows = pl.ds(start, 64)
            result_ref[rows, :] = (
                product_ref[rows, at].astype(jnp.float32)
                + left_ref[rows, :].astype(jnp.float32)
                + right_ref[rows, :].astype(jnp.float32)
            ).astype(jnp.bfloat16)
        rows = pl.ds(part * piece, piece)
        target = (pl.ds(out_ref.shape[0] - height + part * piece, piece), pl.ds(first, width))
        copy = pltpu.make_async_copy(result_ref.at[rows], out_ref.at[target], sem.at[part])
        copy.start()
        copies.append(copy)
    for copy in copies:
        copy.wait()


def finish(result, product, left, right, first):
    inside = pl.BlockSpec(memory_space=pltpu.VMEM)
    anywhere = pl.BlockSpec(memory_space=pl.ANY)
    return pl.pallas_call(
        functools.partial(finish_kernel, first),
        out_shape=jax.ShapeDtypeStruct(result.shape, result.dtype),
        in_specs=[anywhere, inside, inside, inside],
        out_specs=anywhere,
        scratch_shapes=[pltpu.VMEM(left.shape, jnp.bfloat16), pltpu.SemaphoreType.DMA((4,))],
        input_output_aliases={0: 0},
        compiler_params=pltpu.CompilerParams(vmem_limit_bytes=2 << 20),
        name="finish",
    )(result, product, left, right)


def payload_kernel(n, step, product_ref, even_ref, odd_ref, to_even_ref, to_odd_ref):
    me, width = lax.axis_index("tp"), even_ref.shape[1]
    rightward = (lax.rem(me + n - step, n), (me < step).astype(jnp.int32))
    leftward = (lax.rem(me + step, n), (me >= n - step).astype(jnp.int32))
    first = lax.rem(me, 2) == 0
    for flag, source_ref, target_ref in ((first, odd_ref, to_even_ref), (jnp.logical_not(first), even_ref, to_odd_ref)):
        column = jnp.where(flag, rightward[0], leftward[0])
        adds = jnp.where(flag, rightward[1], leftward[1]) > 0
        at = pl.ds(pl.multiple_of(column * width, 128), width)

        @pl.when(adds)
        def _(at=at, source_ref=source_ref, target_ref=target_ref):
            @pl.loop(0, source_ref.shape[0] // 64)
            def _(block):
                rows = pl.ds(pl.multiple_of(block * 64, 64), 64)
                target_ref[rows, :] = source_ref[rows, :] + product_ref[rows, at]

        @pl.when(jnp.logical_not(adds))
        def _(source_ref=source_ref, target_ref=target_ref):
            @pl.loop(0, source_ref.shape[0] // 64)
            def _(block):
                rows = pl.ds(pl.multiple_of(block * 64, 64), 64)
                target_ref[rows, :] = source_ref[rows, :]


def payload(step, product, even, odd):
    inside = pl.BlockSpec(memory_space=pltpu.VMEM)
    return pl.pallas_call(
        functools.partial(payload_kernel, lax.axis_size("tp"), step),
        out_shape=[jax.ShapeDtypeStruct(even.shape, even.dtype)] * 2,
        in_specs=[inside, inside, inside],
        out_specs=[inside, inside],
        compiler_params=pltpu.CompilerParams(vmem_limit_bytes=1 << 20),
        name="payload",
    )(product, even, odd)


def product_kernel(start, columns, rows_ref, weight_ref, out_ref, weight_buf, sems):
    count, _, width = weight_buf.shape
    copies = []
    for group in range(count):
        copy = pltpu.make_async_copy(
            weight_ref.at[:, pl.ds(group * columns + start, width)], weight_buf.at[group], sems.at[group]
        )
        copy.start()
        copies.append(copy)
    for group in range(count):
        copies[group].wait()
        for first in range(0, width, 256):
            step = min(width - first, 256)
            piece = jnp.dot(
                rows_ref[...], weight_buf[group, :, first : first + step], preferred_element_type=jnp.float32
            )
            out_ref[:, group * width + first : group * width + first + step] = piece.astype(jnp.bfloat16)


def local_product(rows, out_weight, start, width):
    n = lax.axis_size("tp")
    height, channels = rows.shape
    columns = out_weight.shape[1] // n
    inside = pl.BlockSpec(memory_space=pltpu.VMEM)
    return pl.pallas_call(
        functools.partial(product_kernel, start, columns),
        out_shape=jax.ShapeDtypeStruct((height, n * width), jnp.bfloat16),
        in_specs=[inside, pl.BlockSpec(memory_space=pl.ANY)],
        out_specs=inside,
        scratch_shapes=[pltpu.VMEM((n, channels, width), jnp.bfloat16), pltpu.SemaphoreType.DMA((n,))],
        compiler_params=pltpu.CompilerParams(vmem_limit_bytes=8 << 20),
        name="local_product",
    )(rows, out_weight)


def exchange(sent, products):
    n, parts = lax.axis_size("tp"), len(sent)
    pairs = [
        [pair for i in range(start, n - 1, 2) for pair in ((i, i + 1), (i + 1, i))] for start in range(2)
    ]
    evens, odds = {}, {}
    for slot in range(1, n + 1):
        for part in range(parts):
            if slot == 1:
                even = odd = sent[part]
            else:
                even, odd = payload(slot - 1, products[part], evens[slot - 1, part], odds[slot - 1, part])
            evens[slot, part] = lax.ppermute(even, "tp", pairs[0])
            odds[slot, part] = lax.ppermute(odd, "tp", pairs[1])
    return evens, odds


def local(queries, keys, values, residues, rates, out_weight, span_order):
    n, ctx = lax.axis_size("tp"), lax.axis_size("ctx")
    tokens, channels = queries.shape
    spans = span_order.shape[0] // ctx
    lined = channels // ctx >= 128 and spans == 2 and ctx & (ctx - 1) == 0 and n & (n - 1) == 0
    totals, gated = span_states(keys, values, rates, spans)
    strips = gather_weights(out_weight) if lined else None
    states = exchange_states(totals) if lined else [lax.all_gather(totals, "ctx", axis=0, tiled=True)]
    conv = functools.partial(convolve, span_order, queries, gated, residues, rates, states, spans)
    if not lined:
        outputs = [conv(span, 0, channels) for span in range(spans)]
        part = jnp.dot(jnp.concatenate(outputs), out_weight, preferred_element_type=jnp.float32)
        return lax.psum_scatter(part.astype(jnp.bfloat16), "tp", scatter_dimension=1, tiled=True)
    lead = channels // 128 * FIRST // 8 * 128
    spots = [(0, lead), (lead, channels - lead)]
    sent, products = [], []
    response = span_response(gated, residues, rates, spans, 0, *spots[0])
    sent.append(complete(span_order, queries, response, residues, rates, states, spans, 0, spots[0][0]))
    for part in range(1, PARTS):
        sent.append(conv(0, *spots[part]))
    rest = conv(1, 0, channels)
    for part, spot in enumerate(spots):
        products.append(local_product(rest, out_weight, *spot))
    evens, odds = exchange(sent, products)
    arrived = [[side[slot, part] for slot in range(1, n) for part in range(PARTS)] for side in (evens, odds)]
    result = upper(out_weight, strips, sent, *arrived, tokens)
    for part in range(PARTS):
        result = finish(result, products[part], evens[n, part], odds[n, part], spots[part][0])
    return result


def solution(mesh):
    placed = (
        P("ctx", "tp"),
        P("ctx", "tp"),
        P("ctx", "tp"),
        P(None, "tp"),
        P(None, "tp"),
        P("tp", None),
        P(),
    )

    return jax.shard_map(local, mesh=mesh, in_specs=placed, out_specs=P("ctx", "tp"), check_vma=False)
```
